128 devices in a mesh: seq: 4 (over y), kv: 32 (over z, x, core).
Axes of the slice: x: 4, y: 4, z: 4, core: 2. Of those that a mesh axis runs over, the one named last changes fastest.
Arguments:
- q_nope: bfloat16 [16, 8, 128, 128], P('seq', None, 'kv'), may hold values from -6 to 6
- q_rope: bfloat16 [16, 8, 128, 64], P('seq', None, 'kv')
- w_uk: bfloat16 [128, 128, 512], P('kv'), may hold values from -0.5 to 0.5
- w_uv: bfloat16 [128, 512, 128], P('kv'), may hold values from -0.25 to 0.25
- cache: bfloat16 [8192, 64, 576], P(('seq', 'kv'))
- page_table: int32 [16, 32, 16], P('seq', 'kv'), may hold values from 0 to 63, as said below
- lengths: int32 [16], P('seq'), may hold values from 2048 to 32768
- draft_kv: bfloat16 [16, 8, 576], P('seq'), may hold values from -6 to 6
- flags: int32 [16, 8], P('seq'), may hold values 0 or 1
Outputs:
- attended: bfloat16 [16, 8, 128, 128], P('seq', None, 'kv')
- accepted: int32 [16], P('seq')
- accepted_total: int32 [], replicated
The draws below stay inside these ranges and needn't reach their ends.
Inputs may be any that keep to these rules, and one draw needn't show every extreme that they name: `page_table`: on every index of seq and kv, the 4 x 16 entries of the page table name each page of that device's pool exactly once.
All inputs are finite; a program needn't handle non-finite values. No bound on the sum of `flags` on one device may be relied on, other than what follows from the above.
Results may differ from the reference program's by a relative error of at most 0.019.
Values may be sent and summed in bfloat16 or wider, within the bound.
A program may use at most 128 MiB of HBM per device.

```python
import jax
import jax.numpy as jnp
from jax import lax

H = 128
LATENT = 512
ROPE = 64
NOPE = 128
VHEAD = 128
DRAFT = 8
PAGE = 64
SEQ_DEV = 4
CTX_DEV = 1024
SEQS = 16
CTX = 32768
PPD = 16
POOL_DEV = 64
POOL = 8192


def draw_q_rope(key, part):
    base = jax.random.truncated_normal(key, -6.0, 6.0, (SEQS, DRAFT, H, ROPE), jnp.float32)
    return base.astype(jnp.bfloat16)


def draw_cache(key, part):
    width = LATENT + ROPE
    base = jax.random.truncated_normal(key, -6.0, 6.0, (POOL, PAGE, width), jnp.float32)
    return base.astype(jnp.bfloat16)


def draw_page_table(key, part):
    groups = SEQS // SEQ_DEV
    kv_count = CTX // CTX_DEV
    keys = jax.random.split(key, groups * kv_count)
    perms = jax.vmap(lambda one: jax.random.permutation(one, POOL_DEV))(keys)
    perms = perms.reshape(groups, kv_count, SEQ_DEV, PPD).transpose(0, 2, 1, 3)
    return perms.reshape(SEQS, kv_count, PPD).astype(jnp.int32)


def with_ends(array, own_key, least, high):
    spot = [jax.random.randint(jax.random.fold_in(own_key, axis), (), 0, length) for axis, length in enumerate(array.shape)]
    widest = array.shape.index(max(array.shape))
    beside = spot[:widest] + [(spot[widest] + 1) % array.shape[widest]] + spot[widest + 1:]
    return array.at[tuple(spot)].set(least).at[tuple(beside)].set(high)


def steps_of(rng, shape, cuts, low, top_value):
    def one(dim, shards_of):
        heights = jax.random.uniform(jax.random.fold_in(jax.random.fold_in(rng, 6), dim), (shards_of,), jnp.float32, low / len(cuts), top_value / len(cuts))
        return jnp.repeat(jnp.exp(heights), shape[dim] // shards_of).reshape((-1,) + (1,) * (len(shape) - dim - 1))

    gain = one(*cuts[0])
    for cut in cuts[1:]:
        gain = gain * one(*cut)
    return gain


def gaussian(rng, extent, scale, reach, pieces=(), held_as=jnp.bfloat16):
    factor_of = steps_of(rng, extent, pieces, -0.22, 0.18) if pieces else 1.0
    result = jax.random.normal(rng, extent, jnp.float32) * scale * factor_of
    return jnp.minimum(jnp.maximum(result, -reach), reach).astype(held_as)


def setup_inputs(seed: int = 0) -> dict:
    splits = jax.random.split(jax.random.key(seed), 10)
    q_nope = gaussian(splits[0], (SEQS, DRAFT, H, NOPE), 1.0, 6.0, ((0, 4), (2, 32)))
    q_rope = draw_q_rope(jax.random.fold_in(splits[9], 71), 0)
    w_uk = gaussian(splits[2], (H, NOPE, LATENT), NOPE ** -0.5, 0.5, ((0, 32),))
    w_uv = gaussian(splits[3], (H, LATENT, VHEAD), LATENT ** -0.5, 0.25, ((0, 32),))
    cache = draw_cache(jax.random.fold_in(splits[9], 71), 0)
    page_table = draw_page_table(jax.random.fold_in(splits[9], 71), 0)
    lengths = with_ends(jax.random.randint(splits[6], (SEQS,), CTX // 16, CTX + 1), jax.random.fold_in(splits[6], 1), CTX // 16, CTX).astype(jnp.int32)
    draft_kv = gaussian(splits[7], (SEQS, DRAFT, LATENT + ROPE), 1.0, 6.0, ((0, 4),))
    flags = with_ends((jax.random.randint(splits[8], (SEQS, DRAFT), 0, 8) < 7).astype(jnp.int32), jax.random.fold_in(splits[8], 1), 0, 1)
    return dict(q_nope=q_nope, q_rope=q_rope, w_uk=w_uk, w_uv=w_uv, cache=cache, page_table=page_table, lengths=lengths, draft_kv=draft_kv, flags=flags)


def reference(q_nope, q_rope, w_uk, w_uv, cache, page_table, lengths, draft_kv, flags):
    latent = w_uk.shape[2]
    scale = (q_nope.shape[-1] + q_rope.shape[-1]) ** -0.5
    q_lat = jnp.einsum('sihn,hnc->sihc', q_nope.astype(jnp.float32), w_uk.astype(jnp.float32)).astype(jnp.bfloat16)
    query = jnp.concatenate([q_lat, q_rope], axis=-1)
    kv_count = page_table.shape[1]
    context = kv_count * CTX_DEV

    def one_sequence(index):
        group = index // SEQ_DEV
        table = page_table[index]
        owners = (group * kv_count + jnp.arange(kv_count, dtype=jnp.int32)[:, None]) * POOL_DEV
        global_pages = (owners + table).reshape(-1).astype(jnp.int32)
        keys = cache[global_pages].reshape(context, cache.shape[2])
        rows = query[index].reshape(DRAFT * H, cache.shape[2])
        score = jnp.dot(rows, keys.T, preferred_element_type=jnp.float32) * scale
        valid = (jnp.arange(context, dtype=jnp.int32) < lengths[index])[None, :]
        score = jnp.where(valid, score, jnp.float32(-1e30))
        peak = jnp.max(score, axis=1)
        weight = jnp.where(valid, jnp.exp(score - peak[:, None]), jnp.float32(0.0))
        denom = jnp.sum(weight, axis=1)
        numer = jnp.dot(weight.astype(jnp.bfloat16), keys[:, :latent], preferred_element_type=jnp.float32)
        drafts = draft_kv[index]
        dscore = jnp.dot(rows, drafts.T, preferred_element_type=jnp.float32) * scale
        position = jnp.arange(DRAFT * H, dtype=jnp.int32) // H
        causal = jnp.arange(DRAFT, dtype=jnp.int32)[None, :] <= position[:, None]
        dpeak = jnp.max(jnp.where(causal, dscore, jnp.float32(-1e30)), axis=1)
        top = jnp.maximum(peak, dpeak)
        factor = jnp.exp(peak - top)
        dweight = jnp.where(causal, jnp.exp(dscore - top[:, None]), jnp.float32(0.0))
        total = denom * factor + jnp.sum(dweight, axis=1)
        mixed = numer * factor[:, None] + jnp.dot(dweight.astype(jnp.bfloat16), drafts[:, :latent], preferred_element_type=jnp.float32)
        return (mixed / total[:, None]).astype(jnp.bfloat16).reshape(DRAFT, H, latent)

    latent_out = lax.map(one_sequence, jnp.arange(q_nope.shape[0], dtype=jnp.int32))
    attended = jnp.einsum('sihc,hcv->sihv', latent_out.astype(jnp.float32), w_uv.astype(jnp.float32)).astype(jnp.bfloat16)
    accepted = jnp.sum(jnp.cumprod(flags, axis=1), axis=1).astype(jnp.int32)
    accepted_total = jnp.sum(accepted).astype(jnp.int32)
    return attended, accepted, accepted_total
```

```python
import functools
import math

import jax
import jax.numpy as jnp
from jax import lax
from jax.experimental import pallas as pl
from jax.experimental.pallas import tpu as pltpu
from jax.sharding import Mesh
from jax.sharding import PartitionSpec as P

KV = ("kv_0", "kv_1", "kv_2")
SEQ_KV = ("seq", "kv_0", "kv_1", "kv_2")
AXES = (("kv_1", "kv_0"), ("kv_0", "kv_1"))
POS = (0, 1, 3, 2)
GROUPS = ((0, 1), (1, 2), (3, 1))
RING = 4
MASKED = -1e30
MESH = pl.DeviceIdType.MESH
NT = (((1,), (1,)), ((), ()))
NN = (((1,), (0,)), ((), ()))


def dot(a, b, dims=NN):
    return lax.dot_general(a, b, dims, preferred_element_type=jnp.float32)


def shifted(axis, by):
    return {axis: lax.rem(lax.axis_index(axis) + by, RING)}


def kernel(
    scale,
    qn_hbm, qr_hbm, wuk_hbm, wuv_hbm, cache_hbm, draft_hbm, pt_ref, len_ref, flags_ref,
    out_ref, acc_ref, tot_ref,
    qn, qr, wuk, wuv, pool, draft, kbuf, qbuf, nsend, nrecv, ssend, srecv,
    csend, crecv, tsend, trecv, nd, md, ld, lo, count, counts,
    in_sem, key_s, key_r, q1_s, q1_r, q2_s, q2_r, n_s, n_r, s_s, s_r, c_s, c_r, t_s, t_r,
    a_s, a_r,
):
    rate = scale * math.log2(math.e)
    rows = qbuf.shape[3]
    latent = nsend.shape[5]
    seqs, ctx = kbuf.shape[0], kbuf.shape[1]
    own_ctx = ctx // 2
    pages, page = pt_ref.shape[2], pool.shape[1]
    heads = wuk.shape[0]
    line = RING * rows
    core = lax.axis_index("kv_2")
    chip = lax.axis_index("kv_0") * RING + lax.axis_index("kv_1")
    partner = {"kv_2": 1 - core}

    small = []
    for i, (src, dst) in enumerate(
        ((qn_hbm, qn), (wuk_hbm, wuk), (qr_hbm, qr), (draft_hbm, draft), (wuv_hbm, wuv))
    ):
        small.append(pltpu.make_async_copy(src, dst, in_sem.at[i]))
    for copy in small[:4]:
        copy.start()
    quarter = pool.shape[0] // 4
    pools = []
    for i in range(4):
        part = pl.ds(i * quarter, quarter)
        pools.append(pltpu.make_async_copy(cache_hbm.at[part], pool.at[part], in_sem.at[5 + i]))
        pools[-1].start()
    small[4].start()

    barrier = pltpu.get_barrier_semaphore()
    peers = [partner] + [
        shifted(axis, by) for axis in ("kv_0", "kv_1", "seq") for by in range(1, RING)
    ]
    for peer in peers:
        pl.semaphore_signal(barrier, inc=1, device_id=peer, device_id_type=MESH)

    def remote(src, dst, send, recv, peer):
        return pltpu.make_async_remote_copy(
            src_ref=src, dst_ref=dst, send_sem=send, recv_sem=recv,
            device_id=peer, device_id_type=MESH,
        )

    mine = jnp.int32(0)
    for s in range(seqs):
        run, total = jnp.int32(1), jnp.int32(0)
        for i in range(flags_ref.shape[1]):
            run = run * flags_ref[s, i]
            total = total + run
        acc_ref[s] = total
        mine = mine + total
    count[...] = jnp.full(count.shape, mine, jnp.int32)

    for copy in small[:4]:
        copy.wait()
    row = lax.broadcasted_iota(jnp.int32, qn.shape, 0)
    qn_f = qn[...].astype(jnp.float32)
    q_lat = jnp.zeros((qn.shape[0], latent), jnp.float32)
    for h in range(heads):
        part = jnp.where(lax.rem(row, heads) == h, qn_f, 0.0).astype(jnp.bfloat16)
        q_lat = q_lat + dot(part, wuk[h])
    q_lat = q_lat.astype(jnp.bfloat16)
    for s in range(seqs):
        h, u = s // 2, s % 2
        qbuf[h, 0, 0, :, u * latent:(u + 1) * latent] = q_lat[s * rows:(s + 1) * rows]
    for h in range(2):
        ropes = [qr[(2 * h + u) * rows:(2 * h + u + 1) * rows] for u in range(2)]
        qbuf[h, 0, 0, :, 2 * latent:] = jnp.concatenate(ropes, axis=1)

    keys_d = draft[:, :latent]
    d_score = dot(q_lat, keys_d, NT) + dot(qr[...], draft[:, latent:], NT)
    per_seq, drafts = qn.shape[0] // seqs, draft.shape[0] // seqs
    r = lax.broadcasted_iota(jnp.int32, d_score.shape, 0)
    c = lax.broadcasted_iota(jnp.int32, d_score.shape, 1)
    seen = (r // per_seq == c // drafts) & (lax.rem(c, drafts) <= lax.rem(r, per_seq) // heads)
    d_score = jnp.where(seen, d_score, MASKED)
    d_top = jnp.max(d_score, axis=1, keepdims=True)
    d_w = jnp.where(seen, jnp.exp2((d_score - d_top) * rate), 0.0)
    md[...] = jnp.broadcast_to(d_top, md.shape)
    ld[...] = jnp.broadcast_to(jnp.sum(d_w, axis=1, keepdims=True), ld.shape)
    nd[...] = dot(d_w.astype(jnp.bfloat16), keys_d)

    pl.semaphore_wait(barrier, len(peers))

    started = []

    def stage_one(h, by):
        copy = remote(
            qbuf.at[h, 0, 0], qbuf.at[h, 0, RING - by], q1_s.at[h, by - 1],
            q1_r.at[h, RING - by - 1], shifted(AXES[h][0], by),
        )
        copy.start()
        started.append(copy)

    def stage_two(h, j, by):
        copy = remote(
            qbuf.at[h, 0, j], qbuf.at[h, POS[RING - by], j], q2_s.at[h, by - 1, j],
            q2_r.at[h, RING - by - 1, j], shifted(AXES[h][1], by),
        )
        copy.start()
        started.append(copy)

    for by in (1, 3, 2):
        for h in range(2):
            stage_one(h, by)
    for by in (3, 1):
        for h in range(2):
            stage_two(h, 0, by)
    tallies = []
    for by in range(1, RING):
        copy = remote(
            count, counts.at[RING - by - 1], a_s.at[by - 1], a_r.at[RING - by - 1],
            shifted("seq", by),
        )
        copy.start()
        tallies.append(copy)

    for copy in pools:
        copy.wait()
    key_copies = []

    def send_keys(s):
        part = pl.ds(core * own_ctx, own_ctx)
        copy = remote(kbuf.at[s, part], kbuf.at[s, part], key_s.at[s], key_r.at[s], partner)
        copy.start()
        key_copies.append(copy)

    for s in range(seqs):
        def place(t, _, s=s):
            tokens = pool[pt_ref[s, 0, t]]
            at = pl.ds(pl.multiple_of(core * own_ctx + t * page, page), page)
            kbuf[s, at, :latent] = tokens[:, :latent]
            rope = tokens[:, latent:]
            none = jnp.zeros_like(rope)
            both = [rope, none] if s % 2 == 0 else [none, rope]
            kbuf[s, at, latent:] = jnp.concatenate(both, axis=1)
            return 0

        lax.fori_loop(0, pages, place, 0)
        if s:
            send_keys(s - 1)

    for j in (1, 3, 2):
        for h in range(2):
            remote(
                qbuf.at[h, 0, j], qbuf.at[h, 0, j], q1_s.at[h, 0], q1_r.at[h, j - 1],
                partner,
            ).wait_recv()
            for by in (3, 1):
                stage_two(h, j, by)
    send_keys(seqs - 1)
    for j in range(RING):
        for h in range(2):
            stage_two(h, j, 2)

    heavy = []

    def compute(h, group):
        first, places = group
        height = places * line
        for place in range(first, first + places):
            slot = POS[place]
            if slot:
                for j in range(RING):
                    dst = qbuf.at[h, place, j]
                    remote(
                        dst, dst, q2_s.at[h, 0, j], q2_r.at[h, slot - 1, j], partner
                    ).wait_recv()

        def one(u, _):
            s = 2 * h + u
            at = pl.ds(pl.multiple_of(u * latent, latent), latent)
            q = qbuf[h, first:first + places, :, :, at].reshape(height, latent)
            qrope = qbuf[h, first:first + places, :, :, 2 * latent:].reshape(height, 128)
            score = dot(q, kbuf[s, :, :latent], NT) + dot(qrope, kbuf[s, :, latent:], NT)
            position = chip * ctx + lax.broadcasted_iota(jnp.int32, (1, ctx), 1)
            valid = position < len_ref[s]
            score = jnp.where(valid, score, MASKED)
            top = jnp.max(score, axis=1, keepdims=True)
            weight = jnp.where(valid, jnp.exp2((score - top) * rate), 0.0)
            total = jnp.sum(weight, axis=1, keepdims=True)
            lane = lax.broadcasted_iota(jnp.int32, (height, 128), 1)
            stats = jnp.transpose(jnp.where(lane == 0, top, total))[:8]
            for k in range(places):
                ssend[h, first + k, u] = stats[:, k * line:(k + 1) * line]
            numer = dot(weight.astype(jnp.bfloat16), kbuf[s, :, :latent])
            numer = numer.astype(jnp.bfloat16).reshape(places, RING, rows, latent)
            nsend[h, first:first + places, :, u] = numer
            return 0

        lax.fori_loop(0, 2, one, 0)
        for place in range(first, first + places):
            slot = POS[place]
            if slot:
                copies = (
                    remote(
                        nsend.at[h, place], nrecv.at[h, RING - slot - 1], n_s.at[h, slot - 1],
                        n_r.at[h, RING - slot - 1], shifted(AXES[h][1], slot),
                    ),
                    remote(
                        ssend.at[h, place], srecv.at[h, RING - slot - 1], s_s.at[h, slot - 1],
                        s_r.at[h, RING - slot - 1], shifted(AXES[h][1], slot),
                    ),
                )
                for copy in copies:
                    copy.start()
                    heavy.append(copy)

    def keys_arrived(s):
        part = pl.ds((1 - core) * own_ctx, own_ctx)
        remote(
            kbuf.at[s, part], kbuf.at[s, part], key_s.at[s], key_r.at[s], partner
        ).wait_recv()

    for g, group in enumerate(GROUPS):
        for h in range(2):
            if g == 0:
                keys_arrived(2 * h)
                keys_arrived(2 * h + 1)
            compute(h, group)

    light = []
    for h in range(2):
        for slot in range(1, RING):
            remote(
                nrecv.at[h, slot - 1], nrecv.at[h, slot - 1], n_s.at[h, 0], n_r.at[h, slot - 1],
                partner,
            ).wait_recv()
            remote(
                srecv.at[h, slot - 1], srecv.at[h, slot - 1], s_s.at[h, 0], s_r.at[h, slot - 1],
                partner,
            ).wait_recv()
        for u in range(2):
            stat = [ssend[h, 0, u]] + [srecv[h, k, u] for k in range(RING - 1)]
            tops = [x[0:1] for x in stat]
            top = functools.reduce(jnp.maximum, tops)
            ws = [jnp.exp2((x - top) * rate) for x in tops]
            total = sum(w * x[1:2] for w, x in zip(ws, stat))
            sub = lax.broadcasted_iota(jnp.int32, (8, line), 0)
            tsend[h, u] = jnp.where(sub == 0, top, total)
            pick = ws[3]
            for k in (2, 1, 0):
                pick = jnp.where(sub == k, ws[k], pick)
            cols = jnp.transpose(pick)
            mixed = jnp.zeros((line, latent), jnp.float32)
            for k in range(RING):
                part = nsend[h, 0, :, u] if k == 0 else nrecv[h, k - 1, :, u]
                part = part.reshape(line, latent).astype(jnp.float32)
                mixed = mixed + cols[:, k:k + 1] * part
            csend[h, :, u] = mixed.astype(jnp.bfloat16).reshape(RING, rows, latent)
        for j in (1, 3, 2):
            copies = (
                remote(
                    csend.at[h, j], crecv.at[h, RING - j - 1], c_s.at[h, j - 1],
                    c_r.at[h, RING - j - 1], shifted(AXES[h][0], j),
                ),
                remote(
                    tsend.at[h], trecv.at[h, RING - j - 1], t_s.at[h, j - 1],
                    t_r.at[h, RING - j - 1], shifted(AXES[h][0], j),
                ),
            )
            for copy in copies:
                copy.start()
                light.append(copy)

    for h in range(2):
        for slot in range(1, RING):
            remote(
                crecv.at[h, slot - 1], crecv.at[h, slot - 1], c_s.at[h, 0], c_r.at[h, slot - 1],
                partner,
            ).wait_recv()
            remote(
                trecv.at[h, slot - 1], trecv.at[h, slot - 1], t_s.at[h, 0], t_r.at[h, slot - 1],
                partner,
            ).wait_recv()
        for u in range(2):
            here = pl.ds((2 * h + u) * rows, rows)
            tops, totals, parts = [md[here, 0:1]], [ld[here, 0:1]], [nd[here]]
            for slot in range(RING):
                j = (RING - slot) % RING
                stat = tsend[h, u] if slot == 0 else trecv[h, slot - 1, u]
                cols = jnp.transpose(stat)[j * rows:(j + 1) * rows]
                tops.append(cols[:, 0:1])
                totals.append(cols[:, 1:2])
                part = csend[h, 0, u] if slot == 0 else crecv[h, slot - 1, u]
                parts.append(part.astype(jnp.float32))
            top = functools.reduce(jnp.maximum, tops)
            ws = [jnp.exp2((x - top) * rate) for x in tops]
            total = sum(w * x for w, x in zip(ws, totals))
            mixed = sum(w * x for w, x in zip(ws, parts))
            lo[here] = (mixed / total).astype(jnp.bfloat16)

    small[4].wait()
    latent_out = lo[...]
    attended = jnp.zeros(out_ref.shape, jnp.float32)
    row = lax.broadcasted_iota(jnp.int32, out_ref.shape, 0)
    for h in range(heads):
        attended = jnp.where(lax.rem(row, heads) == h, dot(latent_out, wuv[h]), attended)
    out_ref[...] = attended.astype(out_ref.dtype)

    for copy in tallies:
        copy.wait_recv()
    everyone = count[...] + counts[0] + counts[1] + counts[2]
    tot_ref[...] = everyone
    for copy in tallies + started + key_copies + heavy + light:
        copy.wait_send()


def body(q_nope, q_rope, w_uk, w_uv, cache, page_table, lengths, draft_kv, flags):
    seqs, drafts, heads, nope = q_nope.shape
    latent, width = w_uk.shape[2], cache.shape[2]
    rope = width - latent
    scale = (nope + rope) ** -0.5
    count = seqs * drafts * heads
    rows = drafts * heads
    ctx = 2 * page_table.shape[2] * cache.shape[1]
    bf16, f32 = jnp.bfloat16, jnp.float32
    hbm = pl.BlockSpec(memory_space=pl.ANY)
    smem = pl.BlockSpec(memory_space=pltpu.SMEM)
    vmem = pl.BlockSpec(memory_space=pltpu.VMEM)
    dma = pltpu.SemaphoreType.DMA
    scratch = [
        pltpu.VMEM((count, nope), bf16),
        pltpu.VMEM((count, rope), bf16),
        pltpu.VMEM(w_uk.shape, bf16),
        pltpu.VMEM(w_uv.shape, bf16),
        pltpu.VMEM(cache.shape, bf16),
        pltpu.VMEM((seqs * drafts, width), bf16),
        pltpu.VMEM((seqs, ctx, latent + 2 * rope), bf16),
        pltpu.VMEM((2, RING, RING, rows, 2 * (latent + rope)), bf16),
        pltpu.VMEM((2, RING, RING, 2, rows, latent), bf16),
        pltpu.VMEM((2, RING - 1, RING, 2, rows, latent), bf16),
        pltpu.VMEM((2, RING, 2, 8, RING * rows), f32),
        pltpu.VMEM((2, RING - 1, 2, 8, RING * rows), f32),
        pltpu.VMEM((2, RING, 2, rows, latent), bf16),
        pltpu.VMEM((2, RING - 1, 2, rows, latent), bf16),
        pltpu.VMEM((2, 2, 8, RING * rows), f32),
        pltpu.VMEM((2, RING - 1, 2, 8, RING * rows), f32),
        pltpu.VMEM((count, latent), f32),
        pltpu.VMEM((count, 128), f32),
        pltpu.VMEM((count, 128), f32),
        pltpu.VMEM((count, latent), bf16),
        pltpu.VMEM((8, 128), jnp.int32),
        pltpu.VMEM((RING - 1, 8, 128), jnp.int32),
        dma((9,)),
        dma((seqs,)), dma((seqs,)),
        dma((2, RING - 1)), dma((2, RING - 1)),
        dma((2, RING - 1, RING)), dma((2, RING - 1, RING)),
        dma((2, RING - 1)), dma((2, RING - 1)),
        dma((2, RING - 1)), dma((2, RING - 1)),
        dma((2, RING - 1)), dma((2, RING - 1)),
        dma((2, RING - 1)), dma((2, RING - 1)),
        dma((RING - 1,)), dma((RING - 1,)),
    ]
    attended, accepted, total = pl.pallas_call(
        functools.partial(kernel, scale),
        out_shape=(
            jax.ShapeDtypeStruct((count, w_uv.shape[2]), bf16),
            jax.ShapeDtypeStruct((seqs,), jnp.int32),
            jax.ShapeDtypeStruct((8, 128), jnp.int32),
        ),
        in_specs=[hbm] * 6 + [smem] * 3,
        out_specs=(vmem, smem, vmem),
        scratch_shapes=scratch,
        compiler_params=pltpu.CompilerParams(
            collective_id=0, has_side_effects=True, vmem_limit_bytes=60 * 1024 * 1024
        ),
        name="verify",
    )(
        q_nope.reshape(count, nope),
        q_rope.reshape(count, rope),
        w_uk,
        w_uv,
        cache,
        draft_kv.reshape(seqs * drafts, width),
        page_table,
        lengths,
        flags,
    )
    return attended.reshape(seqs, drafts, heads, -1), accepted, total[0, 0]


def solution(mesh):
    split = Mesh(mesh.devices.reshape(mesh.shape["seq"], RING, RING, 2), SEQ_KV)
    return jax.shard_map(
        body,
        mesh=split,
        in_specs=(
            P("seq", None, KV, None),
            P("seq", None, KV, None),
            P(KV, None, None),
            P(KV, None, None),
            P(SEQ_KV, None, None),
            P("seq", KV, None),
            P("seq"),
            P("seq", None, None),
            P("seq", None),
        ),
        out_specs=(P("seq", None, KV, None), P("seq"), P()),
        check_vma=False,
    )
```

```python
import functools
import math

import jax
import jax.numpy as jnp
from jax import lax
from jax.experimental import pallas as pl
from jax.experimental.pallas import tpu as pltpu
from jax.sharding import Mesh
from jax.sharding import PartitionSpec as P

KV = ("kv_0", "kv_1", "kv_2")
SEQ_KV = ("seq", "kv_0", "kv_1", "kv_2")
AXES = (("kv_1", "kv_0"), ("kv_0", "kv_1"))
POS = (0, 1, 3, 2)
GROUPS = ((0, 1), (1, 2), (3, 1))
RING = 4
PAIRS = ((0, 0), (0, 1), (1, 0), (1, 1))
MASKED = -1e30
MESH = pl.DeviceIdType.MESH
NT = (((1,), (1,)), ((), ()))
NN = (((1,), (0,)), ((), ()))


def dot(a, b, dims=NN):
    return lax.dot_general(a, b, dims, preferred_element_type=jnp.float32)


def shifted(axis, by):
    return {axis: lax.rem(lax.axis_index(axis) + by, RING)}


def kernel(
    scale,
    qn_hbm, qr_hbm, wuk_hbm, wuv_hbm, cache_hbm, draft_hbm, pt_ref, len_ref, flags_ref,
    out_ref, acc_ref, tot_ref,
    qn, qr, wuk, wuv, pool, draft, kbuf, qbuf, nsend, nrecv, ssend, srecv,
    csend, crecv, tsend, trecv, nd, md, ld, lo, count, counts,
    in_sem, key_s, key_r, q1_s, q1_r, q2_s, q2_r, n_s, n_r, s_s, s_r, c_s, c_r, t_s, t_r,
    a_s, a_r, far_sem,
):
    rate = scale * math.log2(math.e)
    rows = qbuf.shape[3]
    latent = nsend.shape[5]
    seqs, ctx = kbuf.shape[0], kbuf.shape[1]
    own_ctx = ctx // 2
    pages, page = pt_ref.shape[2], pool.shape[1]
    heads = wuk.shape[0]
    line = RING * rows
    core = lax.axis_index("kv_2")
    chip = lax.axis_index("kv_0") * RING + lax.axis_index("kv_1")
    partner = {"kv_2": 1 - core}

    small = []
    for i, (src, dst) in enumerate(
        ((qn_hbm, qn), (wuk_hbm, wuk), (qr_hbm, qr), (draft_hbm, draft), (wuv_hbm, wuv))
    ):
        small.append(pltpu.make_async_copy(src, dst, in_sem.at[i]))
    for copy in small[:4]:
        copy.start()
    quarter = pool.shape[0] // 4
    pools = []
    for i in range(4):
        part = pl.ds(i * quarter, quarter)
        pools.append(pltpu.make_async_copy(cache_hbm.at[part], pool.at[part], in_sem.at[5 + i]))
        pools[-1].start()
    small[4].start()

    barrier = pltpu.get_barrier_semaphore()
    near = [shifted(axis, by) for axis in ("kv_0", "kv_1", "seq") for by in (1, 3)]
    peers = [partner] + near
    for peer in peers:
        pl.semaphore_signal(barrier, inc=1, device_id=peer, device_id_type=MESH)

    def remote(src, dst, send, recv, peer):
        return pltpu.make_async_remote_copy(
            src_ref=src, dst_ref=dst, send_sem=send, recv_sem=recv,
            device_id=peer, device_id_type=MESH,
        )

    mine = jnp.int32(0)
    for s in range(seqs):
        run, total = jnp.int32(1), jnp.int32(0)
        for i in range(flags_ref.shape[1]):
            run = run * flags_ref[s, i]
            total = total + run
        acc_ref[s] = total
        mine = mine + total
    count[...] = jnp.full(count.shape, mine, jnp.int32)

    def arrived(dst, recv):
        remote(dst, dst, in_sem.at[0], recv, partner).wait_recv()

    for copy in small[:4]:
        copy.wait()
    row = lax.broadcasted_iota(jnp.int32, qn.shape, 0)
    qn_f = qn[...].astype(jnp.float32)
    q_lat = jnp.zeros((qn.shape[0], latent), jnp.float32)
    for h in range(heads):
        part = jnp.where(lax.rem(row, heads) == h, qn_f, 0.0).astype(jnp.bfloat16)
        q_lat = q_lat + dot(part, wuk[h])
    q_lat = q_lat.astype(jnp.bfloat16)
    for s in range(seqs):
        h, u = s // 2, s % 2
        qbuf[h, 0, 0, :, u * latent:(u + 1) * latent] = q_lat[s * rows:(s + 1) * rows]
    for h in range(2):
        ropes = [qr[(2 * h + u) * rows:(2 * h + u + 1) * rows] for u in range(2)]
        qbuf[h, 0, 0, :, 2 * latent:] = jnp.concatenate(ropes, axis=1)

    pl.semaphore_wait(barrier, len(peers))
    for peer in near:
        pl.semaphore_signal(far_sem, inc=1, device_id=peer, device_id_type=MESH)

    started = []

    def send(copy):
        copy.start()
        started.append(copy)

    def stage_one(h, by):
        i = by // 2
        send(remote(
            qbuf.at[h, 0, 0], qbuf.at[h, 0, RING - by], q1_s.at[h, i], q1_r.at[h, i],
            shifted(AXES[h][0], by),
        ))

    def stage_one_far(h, by):
        i = by // 2
        half = pl.ds(i * (rows // 2), rows // 2)
        send(remote(
            qbuf.at[h, 0, RING - by, half], qbuf.at[h, 0, 2, half], q1_s.at[h, 2 + i],
            q1_r.at[h, 2 + i], shifted(AXES[h][0], by),
        ))

    def stage_two(h, j, by):
        i = by // 2
        send(remote(
            qbuf.at[h, 0, j], qbuf.at[h, POS[RING - by], j], q2_s.at[h, i, j],
            q2_r.at[h, i, j], shifted(AXES[h][1], by),
        ))

    def stage_two_far(h, j, by):
        send(remote(
            qbuf.at[h, POS[RING - by], j], qbuf.at[h, POS[2], j], q2_s.at[h, 2, j],
            q2_r.at[h, 2, j], shifted(AXES[h][1], by),
        ))

    for h in range(2):
        for by in (1, 3):
            stage_one(h, by)
    for h in range(2):
        for by in (1, 3):
            stage_two(h, 0, by)

    for copy in pools:
        copy.wait()
    key_copies = []

    def send_keys(s):
        part = pl.ds(core * own_ctx, own_ctx)
        copy = remote(kbuf.at[s, part], kbuf.at[s, part], key_s.at[s], key_r.at[s], partner)
        copy.start()
        key_copies.append(copy)

    for s in range(seqs):
        def place(t, _, s=s):
            tokens = pool[pt_ref[s, 0, t]]
            at = pl.ds(pl.multiple_of(core * own_ctx + t * page, page), page)
            kbuf[s, at, :latent] = tokens[:, :latent]
            rope = tokens[:, latent:]
            none = jnp.zeros_like(rope)
            both = [rope, none] if s % 2 == 0 else [none, rope]
            kbuf[s, at, latent:] = jnp.concatenate(both, axis=1)
            return 0

        lax.fori_loop(0, pages, place, 0)
        if s:
            send_keys(s - 1)

    for h in range(2):
        for by in (1, 3):
            arrived(qbuf.at[h, 0, RING - by], q1_r.at[h, by // 2])
            stage_one_far(h, by)
    for h in range(2):
        for by in (1, 3):
            stage_two(h, by, by)
    for h in range(2):
        for by in (1, 3):
            stage_two(h, RING - by, by)
    send_keys(seqs - 1)

    keys_d = draft[:, :latent]
    d_score = dot(q_lat, keys_d, NT) + dot(qr[...], draft[:, latent:], NT)
    per_seq, drafts = qn.shape[0] // seqs, draft.shape[0] // seqs
    r = lax.broadcasted_iota(jnp.int32, d_score.shape, 0)
    c = lax.broadcasted_iota(jnp.int32, d_score.shape, 1)
    seen = (r // per_seq == c // drafts) & (lax.rem(c, drafts) <= lax.rem(r, per_seq) // heads)
    d_score = jnp.where(seen, d_score, MASKED)
    d_top = jnp.max(d_score, axis=1, keepdims=True)
    d_w = jnp.where(seen, jnp.exp2((d_score - d_top) * rate), 0.0)
    md[...] = jnp.broadcast_to(d_top, md.shape)
    ld[...] = jnp.broadcast_to(jnp.sum(d_w, axis=1, keepdims=True), ld.shape)
    nd[...] = dot(d_w.astype(jnp.bfloat16), keys_d)

    for h in range(2):
        for i in range(2):
            half = pl.ds(i * (rows // 2), rows // 2)
            arrived(qbuf.at[h, 0, 2, half], q1_r.at[h, 2 + i])
        for by in (1, 3):
            stage_two(h, 2, by)

    pl.semaphore_wait(far_sem, len(near))
    tallies = []
    for by in range(1, RING):
        copy = remote(
            count, counts.at[RING - by - 1], a_s.at[by - 1], a_r.at[RING - by - 1],
            shifted("seq", by),
        )
        copy.start()
        tallies.append(copy)

    def relay(i):
        for h in range(2):
            for by, js in ((1, (0, 1)), (3, (3, 2))):
                arrived(qbuf.at[h, POS[RING - by], js[i]], q2_r.at[h, by // 2, js[i]])
                stage_two_far(h, js[i], by)

    heavy = []

    def compute(h, group):
        first, places = group
        height = places * line
        for place in range(first, first + places):
            slot = POS[place]
            left = {0: (), 1: (0, 1), 2: (0, 1, 2, 3), 3: (2, 3)}[slot]
            for j in left:
                arrived(qbuf.at[h, place, j], q2_r.at[h, {1: 1, 2: 2, 3: 0}[slot], j])

        def one(u):
            s = 2 * h + u
            at = slice(u * latent, (u + 1) * latent)
            q = qbuf[h, first:first + places, :, :, at].reshape(height, latent)
            qrope = qbuf[h, first:first + places, :, :, 2 * latent:].reshape(height, 128)
            score = dot(q, kbuf[s, :, :latent], NT) + dot(qrope, kbuf[s, :, latent:], NT)
            position = chip * ctx + lax.broadcasted_iota(jnp.int32, (1, ctx), 1)
            valid = position < len_ref[s]
            score = jnp.where(valid, score, MASKED)
            top = jnp.max(score, axis=1, keepdims=True)
            weight = jnp.where(valid, jnp.exp2((score - top) * rate), 0.0)
            total = jnp.sum(weight, axis=1, keepdims=True)
            lane = lax.broadcasted_iota(jnp.int32, (height, 128), 1)
            stats = jnp.transpose(jnp.where(lane == 0, top, total))[:8]
            for k in range(places):
                ssend[h, first + k, u] = stats[:, k * line:(k + 1) * line]
            numer = dot(weight.astype(jnp.bfloat16), kbuf[s, :, :latent])
            numer = numer.astype(jnp.bfloat16).reshape(places, RING, rows, latent)
            nsend[h, first:first + places, u] = numer

        one(0)
        one(1)
        for u in range(2):
            for place in range(first, first + places):
                slot = POS[place]
                if slot:
                    back, peer = RING - slot - 1, shifted(AXES[h][1], slot)
                    copies = (
                        remote(
                            ssend.at[h, place, u], srecv.at[h, back, u], s_s.at[h, slot - 1, u],
                            s_r.at[h, back, u], peer,
                        ),
                        remote(
                            nsend.at[h, place, u], nrecv.at[h, back, u], n_s.at[h, slot - 1, u],
                            n_r.at[h, back, u], peer,
                        ),
                    )
                    for copy in copies:
                        copy.start()
                        heavy.append(copy)

    other = pl.ds((1 - core) * own_ctx, own_ctx)
    for g, group in enumerate(GROUPS):
        for h in range(2):
            if g == 0:
                for s in (2 * h, 2 * h + 1):
                    arrived(kbuf.at[s, other], key_r.at[s])
            compute(h, group)
            if g == 0:
                relay(h)

    light = []
    for h, u in PAIRS:
        for slot in (1, 3, 2):
            arrived(srecv.at[h, slot - 1, u], s_r.at[h, slot - 1, u])
            arrived(nrecv.at[h, slot - 1, u], n_r.at[h, slot - 1, u])
        stat = [ssend[h, 0, u]] + [srecv[h, k, u] for k in range(RING - 1)]
        tops = [x[0:1] for x in stat]
        top = functools.reduce(jnp.maximum, tops)
        ws = [jnp.exp2((x - top) * rate) for x in tops]
        total = sum(w * x[1:2] for w, x in zip(ws, stat))
        sub = lax.broadcasted_iota(jnp.int32, (8, line), 0)
        tsend[h, u] = jnp.where(sub == 0, top, total)
        pick = ws[3]
        for k in (2, 1, 0):
            pick = jnp.where(sub == k, ws[k], pick)
        cols = jnp.transpose(pick)
        mixed = jnp.zeros((line, latent), jnp.float32)
        for k in range(RING):
            part = nsend[h, 0, u] if k == 0 else nrecv[h, k - 1, u]
            part = part.reshape(line, latent).astype(jnp.float32)
            mixed = mixed + cols[:, k:k + 1] * part
        csend[h, u] = mixed.astype(jnp.bfloat16).reshape(RING, rows, latent)
        for j in (2, 1, 3):
            back, peer = RING - j - 1, shifted(AXES[h][0], j)
            copies = (
                remote(
                    tsend.at[h, u], trecv.at[h, back, u], t_s.at[h, j - 1, u],
                    t_r.at[h, back, u], peer,
                ),
                remote(
                    csend.at[h, u, j], crecv.at[h, back, u], c_s.at[h, j - 1, u],
                    c_r.at[h, back, u], peer,
                ),
            )
            for copy in copies:
                copy.start()
                light.append(copy)

    for h, u in PAIRS:
        for slot in range(1, RING):
            arrived(trecv.at[h, slot - 1, u], t_r.at[h, slot - 1, u])
            arrived(crecv.at[h, slot - 1, u], c_r.at[h, slot - 1, u])
        here = pl.ds((2 * h + u) * rows, rows)
        tops, totals, parts = [md[here, 0:1]], [ld[here, 0:1]], [nd[here]]
        for slot in range(RING):
            j = (RING - slot) % RING
            stat = tsend[h, u] if slot == 0 else trecv[h, slot - 1, u]
            cols = jnp.transpose(stat)[j * rows:(j + 1) * rows]
            tops.append(cols[:, 0:1])
            totals.append(cols[:, 1:2])
            part = csend[h, u, 0] if slot == 0 else crecv[h, slot - 1, u]
            parts.append(part.astype(jnp.float32))
        top = functools.reduce(jnp.maximum, tops)
        ws = [jnp.exp2((x - top) * rate) for x in tops]
        total = sum(w * x for w, x in zip(ws, totals))
        mixed = sum(w * x for w, x in zip(ws, parts))
        lo[here] = (mixed / total).astype(jnp.bfloat16)

    small[4].wait()
    latent_out = lo[...]
    attended = jnp.zeros(out_ref.shape, jnp.float32)
    row = lax.broadcasted_iota(jnp.int32, out_ref.shape, 0)
    for h in range(heads):
        attended = jnp.where(lax.rem(row, heads) == h, dot(latent_out, wuv[h]), attended)
    out_ref[...] = attended.astype(out_ref.dtype)

    for copy in tallies:
        copy.wait_recv()
    tot_ref[...] = count[...] + counts[0] + counts[1] + counts[2]
    for copy in tallies + started + key_copies + heavy + light:
        copy.wait_send()


def hand_over(a_ref, n_ref, t_ref, a_out, n_out, t_out):
    a_out[...] = a_ref[...]
    for s in range(n_ref.shape[0]):
        n_out[s] = n_ref[s]
    t_out[0] = jnp.max(t_ref[...])


def body(q_nope, q_rope, w_uk, w_uv, cache, page_table, lengths, draft_kv, flags):
    seqs, drafts, heads, nope = q_nope.shape
    latent, width = w_uk.shape[2], cache.shape[2]
    rope = width - latent
    scale = (nope + rope) ** -0.5
    count = seqs * drafts * heads
    rows = drafts * heads
    ctx = 2 * page_table.shape[2] * cache.shape[1]
    bf16, f32 = jnp.bfloat16, jnp.float32
    hbm = pl.BlockSpec(memory_space=pl.ANY)
    smem = pl.BlockSpec(memory_space=pltpu.SMEM)
    vmem = pl.BlockSpec(memory_space=pltpu.VMEM)
    dma = pltpu.SemaphoreType.DMA
    scratch = [
        pltpu.VMEM((count, nope), bf16),
        pltpu.VMEM((count, rope), bf16),
        pltpu.VMEM(w_uk.shape, bf16),
        pltpu.VMEM(w_uv.shape, bf16),
        pltpu.VMEM(cache.shape, bf16),
        pltpu.VMEM((seqs * drafts, width), bf16),
        pltpu.VMEM((seqs, ctx, latent + 2 * rope), bf16),
        pltpu.VMEM((2, RING, RING, rows, 2 * (latent + rope)), bf16),
        pltpu.VMEM((2, RING, 2, RING, rows, latent), bf16),
        pltpu.VMEM((2, RING - 1, 2, RING, rows, latent), bf16),
        pltpu.VMEM((2, RING, 2, 8, RING * rows), f32),
        pltpu.VMEM((2, RING - 1, 2, 8, RING * rows), f32),
        pltpu.VMEM((2, 2, RING, rows, latent), bf16),
        pltpu.VMEM((2, RING - 1, 2, rows, latent), bf16),
        pltpu.VMEM((2, 2, 8, RING * rows), f32),
        pltpu.VMEM((2, RING - 1, 2, 8, RING * rows), f32),
        pltpu.VMEM((count, latent), f32),
        pltpu.VMEM((count, 128), f32),
        pltpu.VMEM((count, 128), f32),
        pltpu.VMEM((count, latent), bf16),
        pltpu.VMEM((8, 128), jnp.int32),
        pltpu.VMEM((RING - 1, 8, 128), jnp.int32),
        dma((9,)),
        dma((seqs,)), dma((seqs,)),
        dma((2, 4)), dma((2, 4)),
        dma((2, RING - 1, RING)), dma((2, RING - 1, RING)),
        dma((2, RING - 1, 2)), dma((2, RING - 1, 2)),
        dma((2, RING - 1, 2)), dma((2, RING - 1, 2)),
        dma((2, RING - 1, 2)), dma((2, RING - 1, 2)),
        dma((2, RING - 1, 2)), dma((2, RING - 1, 2)),
        dma((RING - 1,)), dma((RING - 1,)),
        pltpu.SemaphoreType.REGULAR,
    ]
    attended, accepted, total = pl.pallas_call(
        functools.partial(kernel, scale),
        out_shape=(
            jax.ShapeDtypeStruct((count, w_uv.shape[2]), bf16),
            jax.ShapeDtypeStruct((seqs,), jnp.int32),
            jax.ShapeDtypeStruct((8, 128), jnp.int32),
        ),
        in_specs=[hbm] * 6 + [smem] * 3,
        out_specs=(vmem, smem, vmem),
        scratch_shapes=scratch,
        compiler_params=pltpu.CompilerParams(
            collective_id=0, has_side_effects=True, vmem_limit_bytes=60 * 1024 * 1024
        ),
        name="verify",
    )(
        q_nope.reshape(count, nope),
        q_rope.reshape(count, rope),
        w_uk,
        w_uv,
        cache,
        draft_kv.reshape(seqs * drafts, width),
        page_table,
        lengths,
        flags,
    )
    attended, accepted, total = pl.pallas_call(
        hand_over,
        out_shape=(
            jax.ShapeDtypeStruct(attended.shape, bf16),
            jax.ShapeDtypeStruct((seqs,), jnp.int32),
            jax.ShapeDtypeStruct((1,), jnp.int32),
        ),
        in_specs=[vmem, smem, vmem],
        out_specs=(vmem, smem, smem),
        name="hand_over",
    )(attended, accepted, total)
    return attended.reshape(seqs, drafts, heads, -1), accepted, total.reshape(())


def solution(mesh):
    split = Mesh(mesh.devices.reshape(mesh.shape["seq"], RING, RING, 2), SEQ_KV)
    return jax.shard_map(
        body,
        mesh=split,
        in_specs=(
            P("seq", None, KV, None),
            P("seq", None, KV, None),
            P(KV, None, None),
            P(KV, None, None),
            P(SEQ_KV, None, None),
            P("seq", KV, None),
            P("seq"),
            P("seq", None, None),
            P("seq", None),
        ),
        out_specs=(P("seq", None, KV, None), P("seq"), P()),
        check_vma=False,
    )
```

```python
import functools
import math

import jax
import jax.numpy as jnp
from jax import lax
from jax.experimental import pallas as pl
from jax.experimental.pallas import tpu as pltpu
from jax.sharding import Mesh
from jax.sharding import PartitionSpec as P

KV = ("kv_0", "kv_1", "kv_2")
SEQ_KV = ("seq", "kv_0", "kv_1", "kv_2")
AXES = (("kv_1", "kv_0"), ("kv_0", "kv_1"))
PLACE = (3, 0, 2, 1)
SLOT = (1, 3, 2, 0)
HOME = PLACE[0]
GROUPS = ((0, 2), (2, 2))
RING = 4
PAIRS = ((0, 0), (1, 0), (0, 1), (1, 1))
MASKED = -1e30
MESH = pl.DeviceIdType.MESH
NT = (((1,), (1,)), ((), ()))
NN = (((1,), (0,)), ((), ()))


def dot(a, b, dims=NN):
    return lax.dot_general(a, b, dims, preferred_element_type=jnp.float32)


def shifted(axis, by):
    return {axis: lax.rem(lax.axis_index(axis) + by, RING)}


def kernel(
    scale,
    qn_hbm, qr_hbm, wuk_hbm, wuv_hbm, cache_hbm, draft_hbm, pt_ref, len_ref, flags_ref,
    out_ref, acc_ref, tot_ref,
    qn, qr, wuk, wuv, pool, draft, kbuf, qbuf, nsend, nrecv, ssend, srecv,
    csend, crecv, tsend, trecv, nd, md, ld, lo, count, counts,
    in_sem, key_s, key_r, q1_s, q1_r, q2_s, q2_r, n_s, n_r, s_s, s_r, c_s, c_r, t_s, t_r,
    a_s, a_r, far_sem,
):
    rate = scale * math.log2(math.e)
    rows = qbuf.shape[3]
    latent = nsend.shape[5]
    seqs, ctx = kbuf.shape[0], kbuf.shape[1]
    own_ctx = ctx // 2
    pages, page = pt_ref.shape[2], pool.shape[1]
    heads = wuk.shape[0]
    line = RING * rows
    core = lax.axis_index("kv_2")
    chip = lax.axis_index("kv_0") * RING + lax.axis_index("kv_1")
    partner = {"kv_2": 1 - core}

    small = []
    for i, (src, dst) in enumerate(
        ((qn_hbm, qn), (wuk_hbm, wuk), (qr_hbm, qr), (draft_hbm, draft), (wuv_hbm, wuv))
    ):
        small.append(pltpu.make_async_copy(src, dst, in_sem.at[i]))
    for copy in small[:4]:
        copy.start()
    quarter = pool.shape[0] // 4
    pools = []
    for i in range(4):
        part = pl.ds(i * quarter, quarter)
        pools.append(pltpu.make_async_copy(cache_hbm.at[part], pool.at[part], in_sem.at[5 + i]))
        pools[-1].start()
    small[4].start()

    barrier = pltpu.get_barrier_semaphore()
    near = [shifted(axis, by) for axis in ("kv_0", "kv_1", "seq") for by in (1, 3)]
    peers = [partner] + near
    for peer in peers:
        pl.semaphore_signal(barrier, inc=1, device_id=peer, device_id_type=MESH)

    def remote(src, dst, send, recv, peer):
        return pltpu.make_async_remote_copy(
            src_ref=src, dst_ref=dst, send_sem=send, recv_sem=recv,
            device_id=peer, device_id_type=MESH,
        )

    mine = jnp.int32(0)
    for s in range(seqs):
        run, total = jnp.int32(1), jnp.int32(0)
        for i in range(flags_ref.shape[1]):
            run = run * flags_ref[s, i]
            total = total + run
        acc_ref[s] = total
        mine = mine + total
    count[...] = jnp.full(count.shape, mine, jnp.int32)

    def arrived(dst, recv):
        remote(dst, dst, in_sem.at[0], recv, partner).wait_recv()

    for copy in small[:4]:
        copy.wait()
    row = lax.broadcasted_iota(jnp.int32, qn.shape, 0)
    qn_f = qn[...].astype(jnp.float32)
    q_lat = jnp.zeros((qn.shape[0], latent), jnp.float32)
    for h in range(heads):
        part = jnp.where(lax.rem(row, heads) == h, qn_f, 0.0).astype(jnp.bfloat16)
        q_lat = q_lat + dot(part, wuk[h])
    q_lat = q_lat.astype(jnp.bfloat16)
    for s in range(seqs):
        h, u = s // 2, s % 2
        qbuf[h, HOME, 0, :, u * latent:(u + 1) * latent] = q_lat[s * rows:(s + 1) * rows]
    for h in range(2):
        ropes = [qr[(2 * h + u) * rows:(2 * h + u + 1) * rows] for u in range(2)]
        qbuf[h, HOME, 0, :, 2 * latent:] = jnp.concatenate(ropes, axis=1)

    pl.semaphore_wait(barrier, len(peers))
    for peer in near:
        pl.semaphore_signal(far_sem, inc=1, device_id=peer, device_id_type=MESH)

    started = []

    def send(copy):
        copy.start()
        started.append(copy)

    def stage_one(h, by):
        i = by // 2
        send(remote(
            qbuf.at[h, HOME, 0], qbuf.at[h, HOME, RING - by], q1_s.at[h, i], q1_r.at[h, i],
            shifted(AXES[h][0], by),
        ))

    def stage_one_far(h, by):
        i = by // 2
        half = pl.ds(i * (rows // 2), rows // 2)
        send(remote(
            qbuf.at[h, HOME, RING - by, half], qbuf.at[h, HOME, 2, half], q1_s.at[h, 2 + i],
            q1_r.at[h, 2 + i], shifted(AXES[h][0], by),
        ))

    def stage_two(h, j, by):
        i = by // 2
        send(remote(
            qbuf.at[h, HOME, j], qbuf.at[h, PLACE[RING - by], j], q2_s.at[h, i, j],
            q2_r.at[h, i, j], shifted(AXES[h][1], by),
        ))

    def stage_two_far(h, j, by):
        send(remote(
            qbuf.at[h, PLACE[RING - by], j], qbuf.at[h, PLACE[2], j], q2_s.at[h, 2, j],
            q2_r.at[h, 2, j], shifted(AXES[h][1], by),
        ))

    for h in range(2):
        for by in (1, 3):
            stage_one(h, by)
    for h in range(2):
        for by in (1, 3):
            stage_two(h, 0, by)

    for copy in pools:
        copy.wait()
    key_copies = []

    def send_keys(s):
        part = pl.ds(core * own_ctx, own_ctx)
        copy = remote(kbuf.at[s, part], kbuf.at[s, part], key_s.at[s], key_r.at[s], partner)
        copy.start()
        key_copies.append(copy)

    for s in range(seqs):
        def place(t, _, s=s):
            tokens = pool[pt_ref[s, 0, t]]
            at = pl.ds(pl.multiple_of(core * own_ctx + t * page, page), page)
            kbuf[s, at, :latent] = tokens[:, :latent]
            rope = tokens[:, latent:]
            none = jnp.zeros_like(rope)
            both = [rope, none] if s % 2 == 0 else [none, rope]
            kbuf[s, at, latent:] = jnp.concatenate(both, axis=1)
            return 0

        lax.fori_loop(0, pages, place, 0)
        if s:
            send_keys(s - 1)

    for h in range(2):
        for by in (1, 3):
            arrived(qbuf.at[h, HOME, RING - by], q1_r.at[h, by // 2])
            stage_one_far(h, by)
    for h in range(2):
        for by in (1, 3):
            stage_two(h, by, by)
    for h in range(2):
        for by in (1, 3):
            stage_two(h, RING - by, by)
    send_keys(seqs - 1)

    keys_d = draft[:, :latent]
    d_score = dot(q_lat, keys_d, NT) + dot(qr[...], draft[:, latent:], NT)
    per_seq, drafts = qn.shape[0] // seqs, draft.shape[0] // seqs
    r = lax.broadcasted_iota(jnp.int32, d_score.shape, 0)
    c = lax.broadcasted_iota(jnp.int32, d_score.shape, 1)
    seen = (r // per_seq == c // drafts) & (lax.rem(c, drafts) <= lax.rem(r, per_seq) // heads)
    d_score = jnp.where(seen, d_score, MASKED)
    d_top = jnp.max(d_score, axis=1, keepdims=True)
    d_w = jnp.where(seen, jnp.exp2((d_score - d_top) * rate), 0.0)
    md[...] = jnp.broadcast_to(d_top, md.shape)
    ld[...] = jnp.broadcast_to(jnp.sum(d_w, axis=1, keepdims=True), ld.shape)
    nd[...] = dot(d_w.astype(jnp.bfloat16), keys_d)

    for h in range(2):
        for i in range(2):
            half = pl.ds(i * (rows // 2), rows // 2)
            arrived(qbuf.at[h, HOME, 2, half], q1_r.at[h, 2 + i])
        for by in (1, 3):
            stage_two(h, 2, by)

    pl.semaphore_wait(far_sem, len(near))
    tallies = []
    for by in range(1, RING):
        copy = remote(
            count, counts.at[RING - by - 1], a_s.at[by - 1], a_r.at[RING - by - 1],
            shifted("seq", by),
        )
        copy.start()
        tallies.append(copy)

    def relay(i):
        for h in range(2):
            for by, js in ((1, (0, 1)), (3, (3, 2))):
                arrived(qbuf.at[h, PLACE[RING - by], js[i]], q2_r.at[h, by // 2, js[i]])
                stage_two_far(h, js[i], by)

    heavy = []

    def arrive_all(h, group):
        first, places = group
        for place in range(first, first + places):
            slot = SLOT[place]
            left = {0: (), 1: (0, 1), 2: (0, 1, 2, 3), 3: (2, 3)}[slot]
            for j in left:
                arrived(qbuf.at[h, place, j], q2_r.at[h, {1: 1, 2: 2, 3: 0}[slot], j])

    def attend(h, u, group):
        first, places = group
        height = places * line
        s = 2 * h + u
        at = slice(u * latent, (u + 1) * latent)
        q = qbuf[h, first:first + places, :, :, at].reshape(height, latent)
        qrope = qbuf[h, first:first + places, :, :, 2 * latent:].reshape(height, 128)
        score = dot(q, kbuf[s, :, :latent], NT) + dot(qrope, kbuf[s, :, latent:], NT)
        position = chip * ctx + lax.broadcasted_iota(jnp.int32, (1, ctx), 1)
        valid = position < len_ref[s]
        score = jnp.where(valid, score, MASKED)
        top = jnp.max(score, axis=1, keepdims=True)
        weight = jnp.where(valid, jnp.exp2((score - top) * rate), 0.0)
        total = jnp.sum(weight, axis=1, keepdims=True)
        lane = lax.broadcasted_iota(jnp.int32, (height, 128), 1)
        stats = jnp.transpose(jnp.where(lane == 0, top, total))[:8]
        for k in range(places):
            ssend[h, first + k, u] = stats[:, k * line:(k + 1) * line]
        numer = dot(weight.astype(jnp.bfloat16), kbuf[s, :, :latent])
        nsend[h, first:first + places, u] = numer.astype(jnp.bfloat16).reshape(
            places, RING, rows, latent
        )

    def send_sums(h, u, place):
        slot = SLOT[place]
        back, peer = RING - slot - 1, shifted(AXES[h][1], slot)
        copies = (
            remote(
                ssend.at[h, place, u], srecv.at[h, back, u], s_s.at[h, slot - 1, u],
                s_r.at[h, back, u], peer,
            ),
            remote(
                nsend.at[h, place, u], nrecv.at[h, back, u], n_s.at[h, slot - 1, u],
                n_r.at[h, back, u], peer,
            ),
        )
        for copy in copies:
            copy.start()
            heavy.append(copy)

    relay(0)
    relay(1)
    other = pl.ds((1 - core) * own_ctx, own_ctx)
    for g, group in enumerate(GROUPS):
        for h in range(2):
            arrive_all(h, group)
        for u in range(2):
            for h in range(2):
                if g == 0:
                    arrived(kbuf.at[2 * h + u, other], key_r.at[2 * h + u])
            for h in range(2):
                attend(h, u, group)
            for h in range(2):
                for place in range(group[0], group[0] + group[1]):
                    if place != HOME:
                        send_sums(h, u, place)

    light = []
    for h, u in PAIRS:
        for slot in (1, 3, 2):
            arrived(srecv.at[h, slot - 1, u], s_r.at[h, slot - 1, u])
            arrived(nrecv.at[h, slot - 1, u], n_r.at[h, slot - 1, u])
        stat = [ssend[h, HOME, u]] + [srecv[h, k, u] for k in range(RING - 1)]
        tops = [x[0:1] for x in stat]
        top = functools.reduce(jnp.maximum, tops)
        ws = [jnp.exp2((x - top) * rate) for x in tops]
        total = sum(w * x[1:2] for w, x in zip(ws, stat))
        sub = lax.broadcasted_iota(jnp.int32, (8, line), 0)
        tsend[h, u] = jnp.where(sub == 0, top, total)
        pick = ws[3]
        for k in (2, 1, 0):
            pick = jnp.where(sub == k, ws[k], pick)
        cols = jnp.transpose(pick)
        mixed = jnp.zeros((line, latent), jnp.float32)
        for k in range(RING):
            part = nsend[h, HOME, u] if k == 0 else nrecv[h, k - 1, u]
            part = part.reshape(line, latent).astype(jnp.float32)
            mixed = mixed + cols[:, k:k + 1] * part
        csend[h, u] = mixed.astype(jnp.bfloat16).reshape(RING, rows, latent)
        for j in (2, 1, 3):
            back, peer = RING - j - 1, shifted(AXES[h][0], j)
            copies = (
                remote(
                    tsend.at[h, u], trecv.at[h, back, u], t_s.at[h, j - 1, u],
                    t_r.at[h, back, u], peer,
                ),
                remote(
                    csend.at[h, u, j], crecv.at[h, back, u], c_s.at[h, j - 1, u],
                    c_r.at[h, back, u], peer,
                ),
            )
            for copy in copies:
                copy.start()
                light.append(copy)

    for h, u in PAIRS:
        for slot in range(1, RING):
            arrived(trecv.at[h, slot - 1, u], t_r.at[h, slot - 1, u])
            arrived(crecv.at[h, slot - 1, u], c_r.at[h, slot - 1, u])
        here = pl.ds((2 * h + u) * rows, rows)
        tops, totals, parts = [md[here, 0:1]], [ld[here, 0:1]], [nd[here]]
        for slot in range(RING):
            j = (RING - slot) % RING
            stat = tsend[h, u] if slot == 0 else trecv[h, slot - 1, u]
            cols = jnp.transpose(stat)[j * rows:(j + 1) * rows]
            tops.append(cols[:, 0:1])
            totals.append(cols[:, 1:2])
            part = csend[h, u, 0] if slot == 0 else crecv[h, slot - 1, u]
            parts.append(part.astype(jnp.float32))
        top = functools.reduce(jnp.maximum, tops)
        ws = [jnp.exp2((x - top) * rate) for x in tops]
        total = sum(w * x for w, x in zip(ws, totals))
        mixed = sum(w * x for w, x in zip(ws, parts))
        lo[here] = (mixed / total).astype(jnp.bfloat16)

    small[4].wait()
    latent_out = lo[...]
    attended = jnp.zeros(out_ref.shape, jnp.float32)
    row = lax.broadcasted_iota(jnp.int32, out_ref.shape, 0)
    for h in range(heads):
        attended = jnp.where(lax.rem(row, heads) == h, dot(latent_out, wuv[h]), attended)
    out_ref[...] = attended.astype(out_ref.dtype)

    for copy in tallies:
        copy.wait_recv()
    tot_ref[...] = count[...] + counts[0] + counts[1] + counts[2]
    for copy in tallies + started + key_copies + heavy + light:
        copy.wait_send()


def hand_over(a_ref, n_ref, t_ref, a_out, n_out, t_out):
    a_out[...] = a_ref[...]
    for s in range(n_ref.shape[0]):
        n_out[s] = n_ref[s]
    t_out[0] = jnp.max(t_ref[...])


def body(q_nope, q_rope, w_uk, w_uv, cache, page_table, lengths, draft_kv, flags):
    seqs, drafts, heads, nope = q_nope.shape
    latent, width = w_uk.shape[2], cache.shape[2]
    rope = width - latent
    scale = (nope + rope) ** -0.5
    count = seqs * drafts * heads
    rows = drafts * heads
    ctx = 2 * page_table.shape[2] * cache.shape[1]
    bf16, f32 = jnp.bfloat16, jnp.float32
    hbm = pl.BlockSpec(memory_space=pl.ANY)
    smem = pl.BlockSpec(memory_space=pltpu.SMEM)
    vmem = pl.BlockSpec(memory_space=pltpu.VMEM)
    dma = pltpu.SemaphoreType.DMA
    scratch = [
        pltpu.VMEM((count, nope), bf16),
        pltpu.VMEM((count, rope), bf16),
        pltpu.VMEM(w_uk.shape, bf16),
        pltpu.VMEM(w_uv.shape, bf16),
        pltpu.VMEM(cache.shape, bf16),
        pltpu.VMEM((seqs * drafts, width), bf16),
        pltpu.VMEM((seqs, ctx, latent + 2 * rope), bf16),
        pltpu.VMEM((2, RING, RING, rows, 2 * (latent + rope)), bf16),
        pltpu.VMEM((2, RING, 2, RING, rows, latent), bf16),
        pltpu.VMEM((2, RING - 1, 2, RING, rows, latent), bf16),
        pltpu.VMEM((2, RING, 2, 8, RING * rows), f32),
        pltpu.VMEM((2, RING - 1, 2, 8, RING * rows), f32),
        pltpu.VMEM((2, 2, RING, rows, latent), bf16),
        pltpu.VMEM((2, RING - 1, 2, rows, latent), bf16),
        pltpu.VMEM((2, 2, 8, RING * rows), f32),
        pltpu.VMEM((2, RING - 1, 2, 8, RING * rows), f32),
        pltpu.VMEM((count, latent), f32),
        pltpu.VMEM((count, 128), f32),
        pltpu.VMEM((count, 128), f32),
        pltpu.VMEM((count, latent), bf16),
        pltpu.VMEM((8, 128), jnp.int32),
        pltpu.VMEM((RING - 1, 8, 128), jnp.int32),
        dma((9,)),
        dma((seqs,)), dma((seqs,)),
        dma((2, 4)), dma((2, 4)),
        dma((2, RING - 1, RING)), dma((2, RING - 1, RING)),
        dma((2, RING - 1, 2)), dma((2, RING - 1, 2)),
        dma((2, RING - 1, 2)), dma((2, RING - 1, 2)),
        dma((2, RING - 1, 2)), dma((2, RING - 1, 2)),
        dma((2, RING - 1, 2)), dma((2, RING - 1, 2)),
        dma((RING - 1,)), dma((RING - 1,)),
        pltpu.SemaphoreType.REGULAR,
    ]
    attended, accepted, total = pl.pallas_call(
        functools.partial(kernel, scale),
        out_shape=(
            jax.ShapeDtypeStruct((count, w_uv.shape[2]), bf16),
            jax.ShapeDtypeStruct((seqs,), jnp.int32),
            jax.ShapeDtypeStruct((8, 128), jnp.int32),
        ),
        in_specs=[hbm] * 6 + [smem] * 3,
        out_specs=(vmem, smem, vmem),
        scratch_shapes=scratch,
        compiler_params=pltpu.CompilerParams(
            collective_id=0, has_side_effects=True, vmem_limit_bytes=60 * 1024 * 1024
        ),
        name="verify",
    )(
        q_nope.reshape(count, nope),
        q_rope.reshape(count, rope),
        w_uk,
        w_uv,
        cache,
        draft_kv.reshape(seqs * drafts, width),
        page_table,
        lengths,
        flags,
    )
    attended, accepted, total = pl.pallas_call(
        hand_over,
        out_shape=(
            jax.ShapeDtypeStruct(attended.shape, bf16),
            jax.ShapeDtypeStruct((seqs,), jnp.int32),
            jax.ShapeDtypeStruct((1,), jnp.int32),
        ),
        in_specs=[vmem, smem, vmem],
        out_specs=(vmem, smem, smem),
        name="hand_over",
    )(attended, accepted, total)
    return attended.reshape(seqs, drafts, heads, -1), accepted, total.reshape(())


def solution(mesh):
    split = Mesh(mesh.devices.reshape(mesh.shape["seq"], RING, RING, 2), SEQ_KV)
    return jax.shard_map(
        body,
        mesh=split,
        in_specs=(
            P("seq", None, KV, None),
            P("seq", None, KV, None),
            P(KV, None, None),
            P(KV, None, None),
            P(SEQ_KV, None, None),
            P("seq", KV, None),
            P("seq"),
            P("seq", None, None),
            P("seq", None),
        ),
        out_specs=(P("seq", None, KV, None), P("seq"), P()),
        check_vma=False,
    )
```

```python
import functools
import math

import jax
import jax.numpy as jnp
from jax import lax
from jax.experimental import pallas as pl
from jax.experimental.pallas import tpu as pltpu
from jax.sharding import Mesh
from jax.sharding import PartitionSpec as P

KV = ("kv_0", "kv_1", "kv_2")
SEQ_KV = ("seq", "kv_0", "kv_1", "kv_2")
AXES = (("kv_1", "kv_0"), ("kv_0", "kv_1"))
PLACE = (3, 0, 2, 1)
SLOT = (1, 3, 2, 0)
HOME = PLACE[0]
GROUPS = ((0, 2), (2, 2))
RING = 4
PAIRS = ((0, 0), (1, 0), (0, 1), (1, 1))
MASKED = -1e30
MESH = pl.DeviceIdType.MESH
NT = (((1,), (1,)), ((), ()))
NN = (((1,), (0,)), ((), ()))


def dot(a, b, dims=NN):
    return lax.dot_general(a, b, dims, preferred_element_type=jnp.float32)


def shifted(axis, by):
    return {axis: lax.rem(lax.axis_index(axis) + by, RING)}


def kernel(
    scale,
    qn_hbm, qr_hbm, wuk_hbm, wuv_hbm, cache_hbm, draft_hbm, pt_hbm, len_hbm, flags_hbm,
    out_ref, acc_ref, tot_ref,
    pt_ref, len_ref, flags_ref, qn, qr, wuk, wuv, pool, draft, kbuf, qbuf, nsend, nrecv, ssend, srecv,
    csend, crecv, tsend, trecv, nd, md, ld, lo, count, counts,
    in_sem, key_s, key_r, q1_s, q1_r, q2_s, q2_r, n_s, n_r, s_s, s_r, c_s, c_r, t_s, t_r,
    a_s, a_r, far_sem,
):
    rate = scale * math.log2(math.e)
    rows = qbuf.shape[3]
    latent = nsend.shape[5]
    seqs, ctx = kbuf.shape[0], kbuf.shape[1]
    own_ctx = ctx // 2
    pages, page = pt_ref.shape[2], pool.shape[1]
    heads = wuk.shape[0]
    line = RING * rows
    core = lax.axis_index("kv_2")
    chip = lax.axis_index("kv_0") * RING + lax.axis_index("kv_1")
    partner = {"kv_2": 1 - core}

    barrier = pltpu.get_barrier_semaphore()
    near = [shifted(axis, by) for axis in ("kv_0", "kv_1", "seq") for by in (1, 3)]
    peers = [partner] + near
    for peer in peers:
        pl.semaphore_signal(barrier, inc=1, device_id=peer, device_id_type=MESH)

    small = []
    for i, (src, dst) in enumerate(
        ((qn_hbm, qn), (wuk_hbm, wuk), (qr_hbm, qr), (draft_hbm, draft), (wuv_hbm, wuv))
    ):
        small.append(pltpu.make_async_copy(src, dst, in_sem.at[i]))
    for copy in small[:4]:
        copy.start()
    quarter = pool.shape[0] // 4
    pools = []
    for i in range(4):
        part = pl.ds(i * quarter, quarter)
        pools.append(pltpu.make_async_copy(cache_hbm.at[part], pool.at[part], in_sem.at[5 + i]))
        pools[-1].start()
    small[4].start()
    tables = []
    for i, (src, dst) in enumerate(((pt_hbm, pt_ref), (len_hbm, len_ref), (flags_hbm, flags_ref))):
        tables.append(pltpu.make_async_copy(src, dst, in_sem.at[9 + i]))
        tables[-1].start()

    def remote(src, dst, send, recv, peer):
        return pltpu.make_async_remote_copy(
            src_ref=src, dst_ref=dst, send_sem=send, recv_sem=recv,
            device_id=peer, device_id_type=MESH,
        )

    def arrived(dst, recv):
        remote(dst, dst, in_sem.at[0], recv, partner).wait_recv()

    for copy in small[:4]:
        copy.wait()
    row = lax.broadcasted_iota(jnp.int32, qn.shape, 0)
    qn_f = qn[...].astype(jnp.float32)
    q_lat = jnp.zeros((qn.shape[0], latent), jnp.float32)
    for h in range(heads):
        part = jnp.where(lax.rem(row, heads) == h, qn_f, 0.0).astype(jnp.bfloat16)
        q_lat = q_lat + dot(part, wuk[h])
    q_lat = q_lat.astype(jnp.bfloat16)
    for s in range(seqs):
        h, u = s // 2, s % 2
        qbuf[h, HOME, 0, :, u * latent:(u + 1) * latent] = q_lat[s * rows:(s + 1) * rows]
    for h in range(2):
        ropes = [qr[(2 * h + u) * rows:(2 * h + u + 1) * rows] for u in range(2)]
        qbuf[h, HOME, 0, :, 2 * latent:] = jnp.concatenate(ropes, axis=1)

    pl.semaphore_wait(barrier, len(peers))
    for peer in near:
        pl.semaphore_signal(far_sem, inc=1, device_id=peer, device_id_type=MESH)

    started = []

    def send(copy):
        copy.start()
        started.append(copy)

    def stage_one(h, by):
        i = by // 2
        send(remote(
            qbuf.at[h, HOME, 0], qbuf.at[h, HOME, RING - by], q1_s.at[h, i], q1_r.at[h, i],
            shifted(AXES[h][0], by),
        ))

    def stage_one_far(h, by):
        i = by // 2
        half = pl.ds(i * (rows // 2), rows // 2)
        send(remote(
            qbuf.at[h, HOME, RING - by, half], qbuf.at[h, HOME, 2, half], q1_s.at[h, 2 + i],
            q1_r.at[h, 2 + i], shifted(AXES[h][0], by),
        ))

    def stage_two(h, j, by):
        i = by // 2
        send(remote(
            qbuf.at[h, HOME, j], qbuf.at[h, PLACE[RING - by], j], q2_s.at[h, i, j],
            q2_r.at[h, i, j], shifted(AXES[h][1], by),
        ))

    def stage_two_far(h, j, by):
        send(remote(
            qbuf.at[h, PLACE[RING - by], j], qbuf.at[h, PLACE[2], j], q2_s.at[h, 2, j],
            q2_r.at[h, 2, j], shifted(AXES[h][1], by),
        ))

    for h in range(2):
        for by in (1, 3):
            stage_one(h, by)
    for h in range(2):
        for by in (1, 3):
            stage_two(h, 0, by)

    for copy in tables:
        copy.wait()

    for copy in pools:
        copy.wait()
    key_copies = []

    def send_keys(s):
        part = pl.ds(core * own_ctx, own_ctx)
        copy = remote(kbuf.at[s, part], kbuf.at[s, part], key_s.at[s], key_r.at[s], partner)
        copy.start()
        key_copies.append(copy)

    for s in range(seqs):
        def place(t, _, s=s):
            tokens = pool[pt_ref[s, 0, t]]
            at = pl.ds(pl.multiple_of(core * own_ctx + t * page, page), page)
            kbuf[s, at, :latent] = tokens[:, :latent]
            rope = tokens[:, latent:]
            none = jnp.zeros_like(rope)
            both = [rope, none] if s % 2 == 0 else [none, rope]
            kbuf[s, at, latent:] = jnp.concatenate(both, axis=1)
            return 0

        lax.fori_loop(0, pages, place, 0)
        if s:
            send_keys(s - 1)

    for h in range(2):
        for by in (1, 3):
            arrived(qbuf.at[h, HOME, RING - by], q1_r.at[h, by // 2])
            stage_one_far(h, by)
    for h in range(2):
        for by in (1, 3):
            stage_two(h, by, by)
    for h in range(2):
        for by in (1, 3):
            stage_two(h, RING - by, by)
    send_keys(seqs - 1)

    mine = jnp.int32(0)
    for s in range(seqs):
        run, total = jnp.int32(1), jnp.int32(0)
        for i in range(flags_ref.shape[1]):
            run = run * flags_ref[s, i]
            total = total + run
        acc_ref[s] = total
        mine = mine + total
    count[...] = jnp.full(count.shape, mine, jnp.int32)

    keys_d = draft[:, :latent]
    d_score = dot(q_lat, keys_d, NT) + dot(qr[...], draft[:, latent:], NT)
    per_seq, drafts = qn.shape[0] // seqs, draft.shape[0] // seqs
    r = lax.broadcasted_iota(jnp.int32, d_score.shape, 0)
    c = lax.broadcasted_iota(jnp.int32, d_score.shape, 1)
    seen = (r // per_seq == c // drafts) & (lax.rem(c, drafts) <= lax.rem(r, per_seq) // heads)
    d_score = jnp.where(seen, d_score, MASKED)
    d_top = jnp.max(d_score, axis=1, keepdims=True)
    d_w = jnp.where(seen, jnp.exp2((d_score - d_top) * rate), 0.0)
    md[...] = jnp.broadcast_to(d_top, md.shape)
    ld[...] = jnp.broadcast_to(jnp.sum(d_w, axis=1, keepdims=True), ld.shape)
    nd[...] = dot(d_w.astype(jnp.bfloat16), keys_d)

    for h in range(2):
        for i in range(2):
            half = pl.ds(i * (rows // 2), rows // 2)
            arrived(qbuf.at[h, HOME, 2, half], q1_r.at[h, 2 + i])
        for by in (1, 3):
            stage_two(h, 2, by)

    pl.semaphore_wait(far_sem, len(near))
    tallies = []
    for by in range(1, RING):
        copy = remote(
            count, counts.at[RING - by - 1], a_s.at[by - 1], a_r.at[RING - by - 1],
            shifted("seq", by),
        )
        copy.start()
        tallies.append(copy)

    def relay(i):
        for h in range(2):
            for by, js in ((1, (0, 1)), (3, (3, 2))):
                arrived(qbuf.at[h, PLACE[RING - by], js[i]], q2_r.at[h, by // 2, js[i]])
                stage_two_far(h, js[i], by)

    heavy = []

    def arrive_all(h, group):
        first, places = group
        for place in range(first, first + places):
            slot = SLOT[place]
            left = {0: (), 1: (0, 1), 2: (0, 1, 2, 3), 3: (2, 3)}[slot]
            for j in left:
                arrived(qbuf.at[h, place, j], q2_r.at[h, {1: 1, 2: 2, 3: 0}[slot], j])

    def attend(h, u, group):
        first, places = group
        height = places * line
        s = 2 * h + u
        at = slice(u * latent, (u + 1) * latent)
        q = qbuf[h, first:first + places, :, :, at].reshape(height, latent)
        qrope = qbuf[h, first:first + places, :, :, 2 * latent:].reshape(height, 128)
        score = dot(q, kbuf[s, :, :latent], NT) + dot(qrope, kbuf[s, :, latent:], NT)
        position = chip * ctx + lax.broadcasted_iota(jnp.int32, (1, ctx), 1)
        valid = position < len_ref[s]
        score = jnp.where(valid, score, MASKED)
        top = jnp.max(score, axis=1, keepdims=True)
        weight = jnp.where(valid, jnp.exp2((score - top) * rate), 0.0)
        total = jnp.sum(weight, axis=1, keepdims=True)
        lane = lax.broadcasted_iota(jnp.int32, (height, 128), 1)
        stats = jnp.transpose(jnp.where(lane == 0, top, total))[:8]
        for k in range(places):
            ssend[h, first + k, u] = stats[:, k * line:(k + 1) * line]
        numer = dot(weight.astype(jnp.bfloat16), kbuf[s, :, :latent])
        nsend[h, first:first + places, u] = numer.astype(jnp.bfloat16).reshape(
            places, RING, rows, latent
        )

    def send_sums(h, u, place):
        slot = SLOT[place]
        back, peer = RING - slot - 1, shifted(AXES[h][1], slot)
        copies = (
            remote(
                ssend.at[h, place, u], srecv.at[h, back, u], s_s.at[h, slot - 1, u],
                s_r.at[h, back, u], peer,
            ),
            remote(
                nsend.at[h, place, u], nrecv.at[h, back, u], n_s.at[h, slot - 1, u],
                n_r.at[h, back, u], peer,
            ),
        )
        for copy in copies:
            copy.start()
            heavy.append(copy)

    relay(0)
    relay(1)
    other = pl.ds((1 - core) * own_ctx, own_ctx)
    for g, group in enumerate(GROUPS):
        for h in range(2):
            arrive_all(h, group)
        for u in range(2):
            for h in range(2):
                if g == 0:
                    arrived(kbuf.at[2 * h + u, other], key_r.at[2 * h + u])
            for h in range(2):
                attend(h, u, group)
            for h in range(2):
                for place in range(group[0], group[0] + group[1]):
                    if place != HOME:
                        send_sums(h, u, place)

    light = []
    for h, u in PAIRS:
        for slot in (1, 3, 2):
            arrived(srecv.at[h, slot - 1, u], s_r.at[h, slot - 1, u])
            arrived(nrecv.at[h, slot - 1, u], n_r.at[h, slot - 1, u])
        stat = [ssend[h, HOME, u]] + [srecv[h, k, u] for k in range(RING - 1)]
        tops = [x[0:1] for x in stat]
        top = functools.reduce(jnp.maximum, tops)
        ws = [jnp.exp2((x - top) * rate) for x in tops]
        total = sum(w * x[1:2] for w, x in zip(ws, stat))
        sub = lax.broadcasted_iota(jnp.int32, (8, line), 0)
        tsend[h, u] = jnp.where(sub == 0, top, total)
        pick = ws[3]
        for k in (2, 1, 0):
            pick = jnp.where(sub == k, ws[k], pick)
        cols = jnp.transpose(pick)
        mixed = jnp.zeros((line, latent), jnp.float32)
        for k in range(RING):
            part = nsend[h, HOME, u] if k == 0 else nrecv[h, k - 1, u]
            part = part.reshape(line, latent).astype(jnp.float32)
            mixed = mixed + cols[:, k:k + 1] * part
        csend[h, u] = mixed.astype(jnp.bfloat16).reshape(RING, rows, latent)
        for j in (2, 1, 3):
            back, peer = RING - j - 1, shifted(AXES[h][0], j)
            copies = (
                remote(
                    tsend.at[h, u], trecv.at[h, back, u], t_s.at[h, j - 1, u],
                    t_r.at[h, back, u], peer,
                ),
                remote(
                    csend.at[h, u, j], crecv.at[h, back, u], c_s.at[h, j - 1, u],
                    c_r.at[h, back, u], peer,
                ),
            )
            for copy in copies:
                copy.start()
                light.append(copy)

    for h, u in PAIRS:
        for slot in range(1, RING):
            arrived(trecv.at[h, slot - 1, u], t_r.at[h, slot - 1, u])
            arrived(crecv.at[h, slot - 1, u], c_r.at[h, slot - 1, u])
        here = pl.ds((2 * h + u) * rows, rows)
        tops, totals, parts = [md[here, 0:1]], [ld[here, 0:1]], [nd[here]]
        for slot in range(RING):
            j = (RING - slot) % RING
            stat = tsend[h, u] if slot == 0 else trecv[h, slot - 1, u]
            cols = jnp.transpose(stat)[j * rows:(j + 1) * rows]
            tops.append(cols[:, 0:1])
            totals.append(cols[:, 1:2])
            part = csend[h, u, 0] if slot == 0 else crecv[h, slot - 1, u]
            parts.append(part.astype(jnp.float32))
        top = functools.reduce(jnp.maximum, tops)
        ws = [jnp.exp2((x - top) * rate) for x in tops]
        total = sum(w * x for w, x in zip(ws, totals))
        mixed = sum(w * x for w, x in zip(ws, parts))
        lo[here] = (mixed / total).astype(jnp.bfloat16)

    small[4].wait()
    latent_out = lo[...]
    attended = jnp.zeros(out_ref.shape, jnp.float32)
    row = lax.broadcasted_iota(jnp.int32, out_ref.shape, 0)
    for h in range(heads):
        attended = jnp.where(lax.rem(row, heads) == h, dot(latent_out, wuv[h]), attended)
    out_ref[...] = attended.astype(out_ref.dtype)

    for copy in tallies:
        copy.wait_recv()
    tot_ref[...] = count[...] + counts[0] + counts[1] + counts[2]
    for copy in tallies + started + key_copies + heavy + light:
        copy.wait_send()


def hand_over(a_ref, n_ref, t_ref, a_out, n_out, t_out):
    a_out[...] = a_ref[...]
    for s in range(n_ref.shape[0]):
        n_out[s] = n_ref[s]
    t_out[0] = jnp.max(t_ref[...])


def body(q_nope, q_rope, w_uk, w_uv, cache, page_table, lengths, draft_kv, flags):
    seqs, drafts, heads, nope = q_nope.shape
    latent, width = w_uk.shape[2], cache.shape[2]
    rope = width - latent
    scale = (nope + rope) ** -0.5
    count = seqs * drafts * heads
    rows = drafts * heads
    ctx = 2 * page_table.shape[2] * cache.shape[1]
    bf16, f32 = jnp.bfloat16, jnp.float32
    hbm = pl.BlockSpec(memory_space=pl.ANY)
    smem = pl.BlockSpec(memory_space=pltpu.SMEM)
    vmem = pl.BlockSpec(memory_space=pltpu.VMEM)
    dma = pltpu.SemaphoreType.DMA
    scratch = [
        pltpu.SMEM(page_table.shape, jnp.int32),
        pltpu.SMEM(lengths.shape, jnp.int32),
        pltpu.SMEM(flags.shape, jnp.int32),
        pltpu.VMEM((count, nope), bf16),
        pltpu.VMEM((count, rope), bf16),
        pltpu.VMEM(w_uk.shape, bf16),
        pltpu.VMEM(w_uv.shape, bf16),
        pltpu.VMEM(cache.shape, bf16),
        pltpu.VMEM((seqs * drafts, width), bf16),
        pltpu.VMEM((seqs, ctx, latent + 2 * rope), bf16),
        pltpu.VMEM((2, RING, RING, rows, 2 * (latent + rope)), bf16),
        pltpu.VMEM((2, RING, 2, RING, rows, latent), bf16),
        pltpu.VMEM((2, RING - 1, 2, RING, rows, latent), bf16),
        pltpu.VMEM((2, RING, 2, 8, RING * rows), f32),
        pltpu.VMEM((2, RING - 1, 2, 8, RING * rows), f32),
        pltpu.VMEM((2, 2, RING, rows, latent), bf16),
        pltpu.VMEM((2, RING - 1, 2, rows, latent), bf16),
        pltpu.VMEM((2, 2, 8, RING * rows), f32),
        pltpu.VMEM((2, RING - 1, 2, 8, RING * rows), f32),
        pltpu.VMEM((count, latent), f32),
        pltpu.VMEM((count, 128), f32),
        pltpu.VMEM((count, 128), f32),
        pltpu.VMEM((count, latent), bf16),
        pltpu.VMEM((8, 128), jnp.int32),
        pltpu.VMEM((RING - 1, 8, 128), jnp.int32),
        dma((12,)),
        dma((seqs,)), dma((seqs,)),
        dma((2, 4)), dma((2, 4)),
        dma((2, RING - 1, RING)), dma((2, RING - 1, RING)),
        dma((2, RING - 1, 2)), dma((2, RING - 1, 2)),
        dma((2, RING - 1, 2)), dma((2, RING - 1, 2)),
        dma((2, RING - 1, 2)), dma((2, RING - 1, 2)),
        dma((2, RING - 1, 2)), dma((2, RING - 1, 2)),
        dma((RING - 1,)), dma((RING - 1,)),
        pltpu.SemaphoreType.REGULAR,
    ]
    attended, accepted, total = pl.pallas_call(
        functools.partial(kernel, scale),
        out_shape=(
            jax.ShapeDtypeStruct((count, w_uv.shape[2]), bf16),
            jax.ShapeDtypeStruct((seqs,), jnp.int32),
            jax.ShapeDtypeStruct((8, 128), jnp.int32),
        ),
        in_specs=[hbm] * 9,
        out_specs=(vmem, smem, vmem),
        scratch_shapes=scratch,
        compiler_params=pltpu.CompilerParams(
            collective_id=0, has_side_effects=True, vmem_limit_bytes=60 * 1024 * 1024
        ),
        name="verify",
    )(
        q_nope.reshape(count, nope),
        q_rope.reshape(count, rope),
        w_uk,
        w_uv,
        cache,
        draft_kv.reshape(seqs * drafts, width),
        page_table,
        lengths,
        flags,
    )
    attended, accepted, total = pl.pallas_call(
        hand_over,
        out_shape=(
            jax.ShapeDtypeStruct(attended.shape, bf16),
            jax.ShapeDtypeStruct((seqs,), jnp.int32),
            jax.ShapeDtypeStruct((1,), jnp.int32),
        ),
        in_specs=[vmem, smem, vmem],
        out_specs=(vmem, smem, smem),
        name="hand_over",
    )(attended, accepted, total)
    return attended.reshape(seqs, drafts, heads, -1), accepted, total.reshape(())


def solution(mesh):
    split = Mesh(mesh.devices.reshape(mesh.shape["seq"], RING, RING, 2), SEQ_KV)
    return jax.shard_map(
        body,
        mesh=split,
        in_specs=(
            P("seq", None, KV, None),
            P("seq", None, KV, None),
            P(KV, None, None),
            P(KV, None, None),
            P(SEQ_KV, None, None),
            P("seq", KV, None),
            P("seq"),
            P("seq", None, None),
            P("seq", None),
        ),
        out_specs=(P("seq", None, KV, None), P("seq"), P()),
        check_vma=False,
    )
```

```python
import functools
import math

import jax
import jax.numpy as jnp
from jax import lax
from jax.experimental import pallas as pl
from jax.experimental.pallas import tpu as pltpu
from jax.sharding import Mesh
from jax.sharding import PartitionSpec as P

KV = ("kv_0", "kv_1", "kv_2")
SEQ_KV = ("seq", "kv_0", "kv_1", "kv_2")
AXES = (("kv_1", "kv_0"), ("kv_0", "kv_1"))
PLACE = (3, 0, 2, 1)
SLOT = (1, 3, 2, 0)
HOME = PLACE[0]
GROUPS = ((0, 2), (2, 2))
RING = 4
PAIRS = ((0, 0), (1, 0), (0, 1), (1, 1))
MASKED = -1e30
MESH = pl.DeviceIdType.MESH
NT = (((1,), (1,)), ((), ()))
NN = (((1,), (0,)), ((), ()))


def dot(a, b, dims=NN):
    return lax.dot_general(a, b, dims, preferred_element_type=jnp.float32)


def shifted(axis, by):
    return {axis: lax.rem(lax.axis_index(axis) + by, RING)}


def kernel(
    scale,
    qn_hbm, qr_hbm, wuk_hbm, wuv_hbm, cache_hbm, draft_hbm, pt_hbm, len_hbm, flags_hbm,
    out_ref, acc_ref, tot_ref,
    pt_ref, len_ref, flags_ref, qn, qr, wuk, wuv, pool, draft, kbuf, qbuf, nsend, nrecv, ssend, srecv,
    csend, crecv, tsend, trecv, nd, md, ld, lo, count, counts,
    in_sem, key_s, key_r, q1_s, q1_r, q2_s, q2_r, n_s, n_r, s_s, s_r, c_s, c_r, t_s, t_r,
    a_s, a_r, far_sem,
):
    rate = scale * math.log2(math.e)
    rows = qbuf.shape[3]
    latent = nsend.shape[5]
    seqs, ctx = kbuf.shape[0], kbuf.shape[1]
    own_ctx = ctx // 2
    pages, page = pt_ref.shape[2], pool.shape[1]
    heads = wuk.shape[0]
    line = RING * rows
    core = lax.axis_index("kv_2")
    chip = lax.axis_index("kv_0") * RING + lax.axis_index("kv_1")
    partner = {"kv_2": 1 - core}

    barrier = pltpu.get_barrier_semaphore()
    near = [shifted(axis, by) for axis in ("kv_0", "kv_1", "seq") for by in (1, 3)]
    peers = [partner] + near
    for peer in peers:
        pl.semaphore_signal(barrier, inc=1, device_id=peer, device_id_type=MESH)

    small = []
    for i, (src, dst) in enumerate(
        ((qn_hbm, qn), (wuk_hbm, wuk), (qr_hbm, qr), (draft_hbm, draft), (wuv_hbm, wuv))
    ):
        small.append(pltpu.make_async_copy(src, dst, in_sem.at[i]))
    for copy in small[:4]:
        copy.start()
    quarter = pool.shape[0] // 4
    pools = []
    for i in range(4):
        part = pl.ds(i * quarter, quarter)
        pools.append(pltpu.make_async_copy(cache_hbm.at[part], pool.at[part], in_sem.at[5 + i]))
        pools[-1].start()
    small[4].start()
    tables = []
    for i, (src, dst) in enumerate(((pt_hbm, pt_ref), (len_hbm, len_ref), (flags_hbm, flags_ref))):
        tables.append(pltpu.make_async_copy(src, dst, in_sem.at[9 + i]))
        tables[-1].start()

    def remote(src, dst, send, recv, peer):
        return pltpu.make_async_remote_copy(
            src_ref=src, dst_ref=dst, send_sem=send, recv_sem=recv,
            device_id=peer, device_id_type=MESH,
        )

    def arrived(dst, recv):
        remote(dst, dst, in_sem.at[0], recv, partner).wait_recv()

    for copy in small[:4]:
        copy.wait()
    row = lax.broadcasted_iota(jnp.int32, qn.shape, 0)
    qn_f = qn[...].astype(jnp.float32)
    q_lat = jnp.zeros((qn.shape[0], latent), jnp.float32)
    for h in range(heads):
        part = jnp.where(lax.rem(row, heads) == h, qn_f, 0.0).astype(jnp.bfloat16)
        q_lat = q_lat + dot(part, wuk[h])
    q_lat = q_lat.astype(jnp.bfloat16)
    for s in range(seqs):
        h, u = s // 2, s % 2
        qbuf[h, HOME, 0, :, u * latent:(u + 1) * latent] = q_lat[s * rows:(s + 1) * rows]
    for h in range(2):
        ropes = [qr[(2 * h + u) * rows:(2 * h + u + 1) * rows] for u in range(2)]
        qbuf[h, HOME, 0, :, 2 * latent:] = jnp.concatenate(ropes, axis=1)

    pl.semaphore_wait(barrier, len(peers))
    for peer in near:
        pl.semaphore_signal(far_sem, inc=1, device_id=peer, device_id_type=MESH)

    started = []

    def send(copy):
        copy.start()
        started.append(copy)

    def stage_one(h, by):
        i = by // 2
        send(remote(
            qbuf.at[h, HOME, 0], qbuf.at[h, HOME, RING - by], q1_s.at[h, i], q1_r.at[h, i],
            shifted(AXES[h][0], by),
        ))

    def stage_one_far(h, by):
        i = by // 2
        half = pl.ds(i * (rows // 2), rows // 2)
        send(remote(
            qbuf.at[h, HOME, RING - by, half], qbuf.at[h, HOME, 2, half], q1_s.at[h, 2 + i],
            q1_r.at[h, 2 + i], shifted(AXES[h][0], by),
        ))

    def stage_two(h, j, by):
        i = by // 2
        send(remote(
            qbuf.at[h, HOME, j], qbuf.at[h, PLACE[RING - by], j], q2_s.at[h, i, j],
            q2_r.at[h, i, j], shifted(AXES[h][1], by),
        ))

    def stage_two_far(h, j, by):
        send(remote(
            qbuf.at[h, PLACE[RING - by], j], qbuf.at[h, PLACE[2], j], q2_s.at[h, 2, j],
            q2_r.at[h, 2, j], shifted(AXES[h][1], by),
        ))

    for h in range(2):
        for by in (1, 3):
            stage_one(h, by)
    for h in range(2):
        for by in (1, 3):
            stage_two(h, 0, by)

    for copy in tables:
        copy.wait()

    for copy in pools:
        copy.wait()
    key_copies = []

    def send_keys(s):
        part = pl.ds(core * own_ctx, own_ctx)
        copy = remote(kbuf.at[s, part], kbuf.at[s, part], key_s.at[s], key_r.at[s], partner)
        copy.start()
        key_copies.append(copy)

    for s in range(seqs):
        def place(t, _, s=s):
            tokens = pool[pt_ref[s, 0, t]]
            at = pl.ds(pl.multiple_of(core * own_ctx + t * page, page), page)
            kbuf[s, at, :latent] = tokens[:, :latent]
            rope = tokens[:, latent:]
            none = jnp.zeros_like(rope)
            both = [rope, none] if s % 2 == 0 else [none, rope]
            kbuf[s, at, latent:] = jnp.concatenate(both, axis=1)
            return 0

        lax.fori_loop(0, pages, place, 0)
        if s:
            send_keys(s - 1)

    for h in range(2):
        for by in (1, 3):
            arrived(qbuf.at[h, HOME, RING - by], q1_r.at[h, by // 2])
            stage_one_far(h, by)
    for h in range(2):
        for by in (1, 3):
            stage_two(h, by, by)
    for h in range(2):
        for by in (1, 3):
            stage_two(h, RING - by, by)
    send_keys(seqs - 1)

    mine = jnp.int32(0)
    for s in range(seqs):
        run, total = jnp.int32(1), jnp.int32(0)
        for i in range(flags_ref.shape[1]):
            run = run * flags_ref[s, i]
            total = total + run
        acc_ref[s] = total
        mine = mine + total
    count[...] = jnp.full(count.shape, mine, jnp.int32)

    keys_d = draft[:, :latent]
    d_score = dot(q_lat, keys_d, NT) + dot(qr[...], draft[:, latent:], NT)
    per_seq, drafts = qn.shape[0] // seqs, draft.shape[0] // seqs
    r = lax.broadcasted_iota(jnp.int32, d_score.shape, 0)
    c = lax.broadcasted_iota(jnp.int32, d_score.shape, 1)
    seen = (r // per_seq == c // drafts) & (lax.rem(c, drafts) <= lax.rem(r, per_seq) // heads)
    d_score = jnp.where(seen, d_score, MASKED)
    d_top = jnp.max(d_score, axis=1, keepdims=True)
    d_w = jnp.where(seen, jnp.exp2((d_score - d_top) * rate), 0.0)
    md[...] = jnp.broadcast_to(d_top, md.shape)
    ld[...] = jnp.broadcast_to(jnp.sum(d_w, axis=1, keepdims=True), ld.shape)
    nd[...] = dot(d_w.astype(jnp.bfloat16), keys_d)

    for h in range(2):
        for i in range(2):
            half = pl.ds(i * (rows // 2), rows // 2)
            arrived(qbuf.at[h, HOME, 2, half], q1_r.at[h, 2 + i])
        for by in (1, 3):
            stage_two(h, 2, by)

    pl.semaphore_wait(far_sem, len(near))
    tallies = []
    for by in range(1, RING):
        copy = remote(
            count, counts.at[RING - by - 1], a_s.at[by - 1], a_r.at[RING - by - 1],
            shifted("seq", by),
        )
        copy.start()
        tallies.append(copy)

    def relay(i):
        for h in range(2):
            for by, js in ((1, (0, 1)), (3, (3, 2))):
                arrived(qbuf.at[h, PLACE[RING - by], js[i]], q2_r.at[h, by // 2, js[i]])
                stage_two_far(h, js[i], by)

    heavy = []

    def arrive_all(h, group):
        first, places = group
        for place in range(first, first + places):
            slot = SLOT[place]
            left = {0: (), 1: (0, 1), 2: (0, 1, 2, 3), 3: (2, 3)}[slot]
            for j in left:
                arrived(qbuf.at[h, place, j], q2_r.at[h, {1: 1, 2: 2, 3: 0}[slot], j])

    def attend(h, u, group):
        first, places = group
        height = places * line
        s = 2 * h + u
        at = slice(u * latent, (u + 1) * latent)
        q = qbuf[h, first:first + places, :, :, at].reshape(height, latent)
        qrope = qbuf[h, first:first + places, :, :, 2 * latent:].reshape(height, 128)
        score = dot(q, kbuf[s, :, :latent], NT) + dot(qrope, kbuf[s, :, latent:], NT)
        position = chip * ctx + lax.broadcasted_iota(jnp.int32, (1, ctx), 1)
        valid = position < len_ref[s]
        score = jnp.where(valid, score, MASKED)
        top = jnp.max(score, axis=1, keepdims=True)
        weight = jnp.where(valid, jnp.exp2((score - top) * rate), 0.0)
        total = jnp.sum(weight, axis=1, keepdims=True)
        lane = lax.broadcasted_iota(jnp.int32, (height, 128), 1)
        stats = jnp.transpose(jnp.where(lane == 0, top, total))[:8]
        for k in range(places):
            ssend[h, first + k, u] = stats[:, k * line:(k + 1) * line]
        numer = dot(weight.astype(jnp.bfloat16), kbuf[s, :, :latent])
        nsend[h, first:first + places, u] = numer.astype(jnp.bfloat16).reshape(
            places, RING, rows, latent
        )

    def send_sums(h, u, place):
        slot = SLOT[place]
        back, peer = RING - slot - 1, shifted(AXES[h][1], slot)
        copies = (
            remote(
                ssend.at[h, place, u], srecv.at[h, back, u], s_s.at[h, slot - 1, u],
                s_r.at[h, back, u], peer,
            ),
            remote(
                nsend.at[h, place, u], nrecv.at[h, back, u], n_s.at[h, slot - 1, u],
                n_r.at[h, back, u], peer,
            ),
        )
        for copy in copies:
            copy.start()
            heavy.append(copy)

    relay(0)
    relay(1)
    other = pl.ds((1 - core) * own_ctx, own_ctx)
    for g, group in enumerate(GROUPS):
        for h in range(2):
            arrive_all(h, group)
        for u in range(2):
            for h in range(2):
                if g == 0:
                    arrived(kbuf.at[2 * h + u, other], key_r.at[2 * h + u])
            last = g == 1 and u == 1
            for h in range(2):
                attend(h, u, (group[0], 1) if last else group)
            for h in range(2):
                for place in range(group[0], group[0] + group[1]):
                    if place != HOME:
                        send_sums(h, u, place)
            if last:
                for h in range(2):
                    attend(h, u, (HOME, 1))

    light = []
    for h, u in PAIRS:
        for slot in (1, 3, 2):
            arrived(srecv.at[h, slot - 1, u], s_r.at[h, slot - 1, u])
            arrived(nrecv.at[h, slot - 1, u], n_r.at[h, slot - 1, u])
        stat = [ssend[h, HOME, u]] + [srecv[h, k, u] for k in range(RING - 1)]
        tops = [x[0:1] for x in stat]
        top = functools.reduce(jnp.maximum, tops)
        ws = [jnp.exp2((x - top) * rate) for x in tops]
        total = sum(w * x[1:2] for w, x in zip(ws, stat))
        sub = lax.broadcasted_iota(jnp.int32, (8, line), 0)
        tsend[h, u] = jnp.where(sub == 0, top, total)
        pick = ws[3]
        for k in (2, 1, 0):
            pick = jnp.where(sub == k, ws[k], pick)
        cols = jnp.transpose(pick)
        mixed = jnp.zeros((line, latent), jnp.float32)
        for k in range(RING):
            part = nsend[h, HOME, u] if k == 0 else nrecv[h, k - 1, u]
            part = part.reshape(line, latent).astype(jnp.float32)
            mixed = mixed + cols[:, k:k + 1] * part
        csend[h, u] = mixed.astype(jnp.bfloat16).reshape(RING, rows, latent)
        for j in (2, 1, 3):
            back, peer = RING - j - 1, shifted(AXES[h][0], j)
            copies = (
                remote(
                    tsend.at[h, u], trecv.at[h, back, u], t_s.at[h, j - 1, u],
                    t_r.at[h, back, u], peer,
                ),
                remote(
                    csend.at[h, u, j], crecv.at[h, back, u], c_s.at[h, j - 1, u],
                    c_r.at[h, back, u], peer,
                ),
            )
            for copy in copies:
                copy.start()
                light.append(copy)

    for h, u in PAIRS:
        for slot in range(1, RING):
            arrived(trecv.at[h, slot - 1, u], t_r.at[h, slot - 1, u])
            arrived(crecv.at[h, slot - 1, u], c_r.at[h, slot - 1, u])
        here = pl.ds((2 * h + u) * rows, rows)
        tops, totals, parts = [md[here, 0:1]], [ld[here, 0:1]], [nd[here]]
        for slot in range(RING):
            j = (RING - slot) % RING
            stat = tsend[h, u] if slot == 0 else trecv[h, slot - 1, u]
            cols = jnp.transpose(stat)[j * rows:(j + 1) * rows]
            tops.append(cols[:, 0:1])
            totals.append(cols[:, 1:2])
            part = csend[h, u, 0] if slot == 0 else crecv[h, slot - 1, u]
            parts.append(part.astype(jnp.float32))
        top = functools.reduce(jnp.maximum, tops)
        ws = [jnp.exp2((x - top) * rate) for x in tops]
        total = sum(w * x for w, x in zip(ws, totals))
        mixed = sum(w * x for w, x in zip(ws, parts))
        lo[here] = (mixed / total).astype(jnp.bfloat16)

    small[4].wait()
    latent_out = lo[...]
    attended = jnp.zeros(out_ref.shape, jnp.float32)
    row = lax.broadcasted_iota(jnp.int32, out_ref.shape, 0)
    for h in range(heads):
        attended = jnp.where(lax.rem(row, heads) == h, dot(latent_out, wuv[h]), attended)
    out_ref[...] = attended.astype(out_ref.dtype)

    for copy in tallies:
        copy.wait_recv()
    tot_ref[...] = count[...] + counts[0] + counts[1] + counts[2]
    for copy in tallies + started + key_copies + heavy + light:
        copy.wait_send()


def hand_over(a_ref, n_ref, t_ref, a_out, n_out, t_out):
    a_out[...] = a_ref[...]
    for s in range(n_ref.shape[0]):
        n_out[s] = n_ref[s]
    t_out[0] = jnp.max(t_ref[...])


def body(q_nope, q_rope, w_uk, w_uv, cache, page_table, lengths, draft_kv, flags):
    seqs, drafts, heads, nope = q_nope.shape
    latent, width = w_uk.shape[2], cache.shape[2]
    rope = width - latent
    scale = (nope + rope) ** -0.5
    count = seqs * drafts * heads
    rows = drafts * heads
    ctx = 2 * page_table.shape[2] * cache.shape[1]
    bf16, f32 = jnp.bfloat16, jnp.float32
    hbm = pl.BlockSpec(memory_space=pl.ANY)
    smem = pl.BlockSpec(memory_space=pltpu.SMEM)
    vmem = pl.BlockSpec(memory_space=pltpu.VMEM)
    dma = pltpu.SemaphoreType.DMA
    scratch = [
        pltpu.SMEM(page_table.shape, jnp.int32),
        pltpu.SMEM(lengths.shape, jnp.int32),
        pltpu.SMEM(flags.shape, jnp.int32),
        pltpu.VMEM((count, nope), bf16),
        pltpu.VMEM((count, rope), bf16),
        pltpu.VMEM(w_uk.shape, bf16),
        pltpu.VMEM(w_uv.shape, bf16),
        pltpu.VMEM(cache.shape, bf16),
        pltpu.VMEM((seqs * drafts, width), bf16),
        pltpu.VMEM((seqs, ctx, latent + 2 * rope), bf16),
        pltpu.VMEM((2, RING, RING, rows, 2 * (latent + rope)), bf16),
        pltpu.VMEM((2, RING, 2, RING, rows, latent), bf16),
        pltpu.VMEM((2, RING - 1, 2, RING, rows, latent), bf16),
        pltpu.VMEM((2, RING, 2, 8, RING * rows), f32),
        pltpu.VMEM((2, RING - 1, 2, 8, RING * rows), f32),
        pltpu.VMEM((2, 2, RING, rows, latent), bf16),
        pltpu.VMEM((2, RING - 1, 2, rows, latent), bf16),
        pltpu.VMEM((2, 2, 8, RING * rows), f32),
        pltpu.VMEM((2, RING - 1, 2, 8, RING * rows), f32),
        pltpu.VMEM((count, latent), f32),
        pltpu.VMEM((count, 128), f32),
        pltpu.VMEM((count, 128), f32),
        pltpu.VMEM((count, latent), bf16),
        pltpu.VMEM((8, 128), jnp.int32),
        pltpu.VMEM((RING - 1, 8, 128), jnp.int32),
        dma((12,)),
        dma((seqs,)), dma((seqs,)),
        dma((2, 4)), dma((2, 4)),
        dma((2, RING - 1, RING)), dma((2, RING - 1, RING)),
        dma((2, RING - 1, 2)), dma((2, RING - 1, 2)),
        dma((2, RING - 1, 2)), dma((2, RING - 1, 2)),
        dma((2, RING - 1, 2)), dma((2, RING - 1, 2)),
        dma((2, RING - 1, 2)), dma((2, RING - 1, 2)),
        dma((RING - 1,)), dma((RING - 1,)),
        pltpu.SemaphoreType.REGULAR,
    ]
    attended, accepted, total = pl.pallas_call(
        functools.partial(kernel, scale),
        out_shape=(
            jax.ShapeDtypeStruct((count, w_uv.shape[2]), bf16),
            jax.ShapeDtypeStruct((seqs,), jnp.int32),
            jax.ShapeDtypeStruct((8, 128), jnp.int32),
        ),
        in_specs=[hbm] * 9,
        out_specs=(vmem, smem, vmem),
        scratch_shapes=scratch,
        compiler_params=pltpu.CompilerParams(
            collective_id=0, has_side_effects=True, vmem_limit_bytes=60 * 1024 * 1024
        ),
        name="verify",
    )(
        q_nope.reshape(count, nope),
        q_rope.reshape(count, rope),
        w_uk,
        w_uv,
        cache,
        draft_kv.reshape(seqs * drafts, width),
        page_table,
        lengths,
        flags,
    )
    attended, accepted, total = pl.pallas_call(
        hand_over,
        out_shape=(
            jax.ShapeDtypeStruct(attended.shape, bf16),
            jax.ShapeDtypeStruct((seqs,), jnp.int32),
            jax.ShapeDtypeStruct((1,), jnp.int32),
        ),
        in_specs=[vmem, smem, vmem],
        out_specs=(vmem, smem, smem),
        name="hand_over",
    )(attended, accepted, total)
    return attended.reshape(seqs, drafts, heads, -1), accepted, total.reshape(())


def solution(mesh):
    split = Mesh(mesh.devices.reshape(mesh.shape["seq"], RING, RING, 2), SEQ_KV)
    return jax.shard_map(
        body,
        mesh=split,
        in_specs=(
            P("seq", None, KV, None),
            P("seq", None, KV, None),
            P(KV, None, None),
            P(KV, None, None),
            P(SEQ_KV, None, None),
            P("seq", KV, None),
            P("seq"),
            P("seq", None, None),
            P("seq", None),
        ),
        out_specs=(P("seq", None, KV, None), P("seq"), P()),
        check_vma=False,
    )
```
